512 devices in a mesh: rep: 4 (over z_hi), dp: 16 (over y, core), tensor: 8 (over x, z_lo).
Axes of the slice: x: 4, y: 8, z: 8 (z_hi: 4, z_lo: 2; z = z_hi * 2 + z_lo), core: 2. Of those that a mesh axis runs over, the one named last changes fastest.
Arguments:
- grad_proj: float32 [64, 3072, 1536], P(('rep', 'dp'), 'tensor'), as said below
- grad_conv: float32 [64, 4, 3328], P(('rep', 'dp'), None, 'tensor'), may hold values from -24 to 24
- param_proj: float32 [3072, 1536], P('tensor', 'dp'), may hold values from -6 to 6
- m_proj: float32 [3072, 1536], P('tensor', 'dp'), may hold values from -2 to 2
- v_proj: float32 [3072, 1536], P('tensor', 'dp'), may hold values from 0.02 to 0.2
- ema_proj: float32 [3072, 1536], P(('tensor', 'dp')), may hold values from -6 to 6
- param_conv: float32 [4, 3328], P(None, 'tensor'), may hold values from -3 to 3
- m_conv: float32 [4, 3328], P(None, 'tensor'), may hold values from -2 to 2
- v_conv: float32 [4, 3328], P(None, 'tensor'), may hold values from 0.02 to 0.2
Outputs:
- new_param_proj: float32 [3072, 1536], P('tensor', 'dp')
- new_m_proj: float32 [3072, 1536], P('tensor', 'dp')
- new_v_proj: float32 [3072, 1536], P('tensor', 'dp')
- new_ema_proj: float32 [3072, 1536], P(('tensor', 'dp'))
- weights_proj: bfloat16 [3072, 1536], P('tensor')
- new_param_conv: float32 [4, 3328], P(None, 'tensor')
- new_m_conv: float32 [4, 3328], P(None, 'tensor')
- new_v_conv: float32 [4, 3328], P(None, 'tensor')
The draws below stay inside these ranges and needn't reach their ends.
Inputs may be any that keep to these rules, and one draw needn't show every extreme that they name: `grad_proj`: Real-valued gradients with entries of magnitude below 3100.
All inputs are finite; a program needn't handle non-finite values.
Results may differ from the reference program's by a relative error of at most 0.001.
Values may be sent and summed in bfloat16 or wider, within the bound.
A program may use at most 64 MiB of HBM per device.

```python
import math
import jax
import jax.numpy as jnp
from jax import lax

D = 1536
INNER = 3072
CONV = 3328
KCONV = 4
REPLICAS = 64


def draw_grad_proj(key, part):
    key_noise, key_rows, key_cols = jax.random.split(key, 3)
    row_trend = jnp.exp(jnp.log(3.0) * jnp.arange(INNER, dtype=jnp.float32) / INNER)
    col_trend = jnp.exp(jnp.log(3.0) * jnp.arange(D, dtype=jnp.float32) / D)
    row_scale = jnp.exp(jax.random.uniform(key_rows, (INNER,), jnp.float32) * jnp.log(10.0)) * row_trend
    col_scale = jnp.exp(jax.random.uniform(key_cols, (D,), jnp.float32) * jnp.log(10.0)) * col_trend
    noise = jnp.clip(jax.random.normal(key_noise, (REPLICAS, INNER, D), jnp.float32), -5.0, 5.0)
    return (0.5 * noise * row_scale[None, :, None] * col_scale[None, None, :]).astype(jnp.float32)


def levels(key, shape, cuts, smallest, top_value):
    level = 1.0
    for dim, shards_of in cuts:
        draws = jax.random.uniform(jax.random.fold_in(jax.random.fold_in(key, 6), dim), (shards_of,), jnp.float32, smallest / len(cuts), top_value / len(cuts))
        level = level * jnp.repeat(jnp.exp(draws), shape[dim] // shards_of).reshape((-1,) + (1,) * (len(shape) - 1 - dim))
    return level


def bell_draw(stream_key, extent, width, limit, pieces=(), held_as=jnp.bfloat16):
    level = levels(stream_key, extent, pieces, -0.22, 0.18) if pieces else 1.0
    drawn = jax.random.normal(stream_key, extent, jnp.float32) * width * level
    return jnp.minimum(jnp.maximum(drawn, -limit), limit).astype(held_as)


def setup_inputs(seed: int = 0) -> dict:
    key_of = jax.random.split(jax.random.key(seed), 10)
    return {
        "grad_proj": draw_grad_proj(jax.random.fold_in(key_of[9], 71), 0),
        "grad_conv": bell_draw(key_of[1], (REPLICAS, KCONV, CONV), 4.0, 24.0, ((0, 64), (2, 8)), jnp.float32),
        "param_proj": bell_draw(key_of[2], (INNER, D), 1.0, 6.0, ((0, 8), (1, 16)), jnp.float32),
        "m_proj": bell_draw(key_of[3], (INNER, D), 0.3, 2.0, ((0, 8), (1, 16)), jnp.float32),
        "v_proj": jnp.clip(jnp.exp(math.log(0.2) - 2.3025851 * jax.random.uniform(key_of[4], (INNER, D), jnp.float32) ** levels(key_of[4], (INNER, D), ((0, 8), (1, 16)), -0.2, 0.2)), 0.02, 0.2),
        "ema_proj": bell_draw(key_of[5], (INNER, D), 1.0, 6.0, ((0, 128),), jnp.float32),
        "param_conv": bell_draw(key_of[6], (KCONV, CONV), 0.5, 3.0, ((1, 8),), jnp.float32),
        "m_conv": bell_draw(key_of[7], (KCONV, CONV), 0.3, 2.0, ((1, 8),), jnp.float32),
        "v_conv": jnp.clip(jnp.exp(math.log(0.2) - 2.3025851 * jax.random.uniform(key_of[8], (KCONV, CONV), jnp.float32) ** levels(key_of[8], (KCONV, CONV), ((1, 8),), -0.2, 0.2)), 0.02, 0.2),
    }


def adamw_step(param_in, first_in, second_in, grad_in):
    first_out = 0.9 * first_in + 0.1 * grad_in
    second_out = 0.95 * second_in + 0.05 * grad_in * grad_in
    bias_one = 1.0 - 0.9 ** 10
    bias_two = 1.0 - 0.95 ** 10
    update = first_out / bias_one / (jnp.sqrt(second_out / bias_two) + 1e-08)
    param_out = param_in - 0.25 * (update + 0.1 * param_in)
    return (param_out, first_out, second_out)

def reference(grad_proj, grad_conv, param_proj, m_proj, v_proj, ema_proj, param_conv, m_conv, v_conv):
    replica_count = grad_proj.shape[0]
    avg_proj = lax.optimization_barrier(jnp.sum(grad_proj, axis=0)) / replica_count
    avg_conv = lax.optimization_barrier(jnp.sum(grad_conv, axis=0)) / replica_count
    grad_norm = jnp.sqrt(jnp.sum(avg_proj * avg_proj) + jnp.sum(avg_conv * avg_conv))
    clip_limit = 0.5 * math.sqrt(INNER * D + KCONV * CONV)
    clip_factor = jnp.minimum(1.0, clip_limit / (grad_norm + 1e-06))
    new_param_proj, new_m_proj, new_v_proj = adamw_step(param_proj, m_proj, v_proj, clip_factor * avg_proj)
    new_param_conv, new_m_conv, new_v_conv = adamw_step(param_conv, m_conv, v_conv, clip_factor * avg_conv)
    weights_proj = new_param_proj.astype(jnp.bfloat16)
    new_ema_proj = 0.9 * ema_proj + 0.1 * new_param_proj
    return (new_param_proj, new_m_proj, new_v_proj, new_ema_proj, weights_proj, new_param_conv, new_m_conv, new_v_conv)
```

```python
import functools
import math

import jax
import jax.numpy as jnp
from jax import lax
from jax.experimental import pallas as pl
from jax.experimental.pallas import tpu as pltpu
from jax.sharding import PartitionSpec as P

D = 1536
INNER = 3072
CONV = 3328
KCONV = 4

F32 = jnp.float32
BF16 = jnp.bfloat16
MESH = pl.DeviceIdType.MESH

YS = 8
REPS = 4
TENS = 8
ROWS = INNER // TENS
BLK = D // (2 * YS)
HALF = BLK // 2
QUART = BLK // REPS
CCOL = CONV // TENS
EROW = ROWS // (2 * YS)
SCALE_UP = 2.0**15
SCALE_DOWN = 2.0**-15


def adamw_step(param_in, first_in, second_in, grad_in):
    first_out = 0.9 * first_in + 0.1 * grad_in
    second_out = 0.95 * second_in + 0.05 * grad_in * grad_in
    bias_one = 1.0 - 0.9**10
    bias_two = 1.0 - 0.95**10
    update = first_out / bias_one / (jnp.sqrt(second_out / bias_two) + 1e-08)
    param_out = param_in - 0.25 * (update + 0.1 * param_in)
    return (param_out, first_out, second_out)


def clip_from(square_sum):
    clip_limit = 0.5 * math.sqrt(INNER * D + KCONV * CONV)
    return jnp.minimum(1.0, clip_limit / (jnp.sqrt(square_sum) + 1e-06))


def encode(x):
    wide = x * SCALE_UP
    square = wide * wide
    return ((square * wide) * jnp.abs(wide)).astype(BF16)


def signed_root(x):
    return x * lax.rsqrt(jnp.maximum(jnp.abs(x), 1e-37))


def decode(code):
    return signed_root(signed_root(code.astype(F32))) * SCALE_DOWN


def fold(x):
    total = x[0:8, 0:128]
    for i in range(x.shape[0] // 8):
        for j in range(x.shape[1] // 128):
            if i or j:
                total = total + x[8 * i : 8 * i + 8, 128 * j : 128 * j + 128]
    return total


P0, M1, P1, M0 = 0, 4, 8, 11
STREAMS = ((P0, 1, 0, 4), (M1, -1, 1, 4), (P1, 1, 1, 3), (M0, -1, 0, 3))


def kernel(
    grad, conv, param, mom, vel, ema, cparam, cmom, cvel,
    o_param, o_mom, o_vel, o_ema, o_weights, o_cparam, o_cmom, o_cvel,
    g_in, gt, pair_out, pair_in, ring_out, ring_in, zq_out, zq_in, zg, wt,
    p_v, m_v, v_v, e_v, conv_y, conv_c, conv_z, cp_v, cm_v, cv_v, norm_r, norm_d, norm_t,
    load_sem, pair_s, pair_r, ring_s, ring_r, zq_s, zq_r, zg_s, zg_r,
    gather_s, gather_r, share_s, share_r, cy_s, cy_r, cc_s, cc_r, cz_s, cz_r,
    nr_s, nr_r, nd_s, nd_r, nt_s, nt_r,
):
    rep = lax.axis_index("rep")
    dp = lax.axis_index("dp")
    ten = lax.axis_index("tensor")
    y = dp // 2
    core = dp % 2
    partner = 2 * y + (1 - core)

    def y_at(off):
        return (y + (off + YS)) % YS

    def remote(src, dst, send, recv, **device):
        return pltpu.make_async_remote_copy(
            src_ref=src, dst_ref=dst, send_sem=send, recv_sem=recv,
            device_id=device, device_id_type=MESH,
        )

    base = (y // 2 + 2) % 4
    turn = 2 * (y % 2) - 1
    order = (base, (base + turn + 4) % 4, (base - turn + 4) % 4, (base + 2) % 4)
    loads = []
    for i, group in enumerate(order):
        cols = pl.ds(pl.multiple_of(group * 384, 128), 384)
        loads.append(pltpu.make_async_copy(grad.at[:, cols], g_in.at[:, cols], load_sem.at[i]))
        loads[-1].start()
    conv_load = pltpu.make_async_copy(conv, conv_y.at[y], load_sem.at[4])
    conv_load.start()
    late = []
    for i, (src, dst) in enumerate(
        ((param, p_v), (mom, m_v), (vel, v_v), (ema, e_v), (cparam, cp_v), (cmom, cm_v), (cvel, cv_v))
    ):
        late.append(pltpu.make_async_copy(src, dst, load_sem.at[5 + i]))
        late[-1].start()

    barrier = pltpu.get_barrier_semaphore()

    def greet(axis, me, count):
        def step(i, carry):
            pl.semaphore_signal(
                barrier, inc=1, device_id={axis: (me + i) % count}, device_id_type=MESH
            )
            return carry

        lax.fori_loop(1, count, step, 0)

    greet("dp", dp, 2 * YS)
    greet("rep", rep, REPS)
    greet("tensor", ten, TENS)

    def turn_group(i):
        loads[i].wait()
        group = order[i]

        def step(j, carry):
            at = pl.multiple_of(group * 384 + j * 128, 128)
            gt[pl.ds(at, 128), :] = g_in[:, pl.ds(at, 128)].T
            return carry

        lax.fori_loop(0, 3, step, 0)
        for k in range(2):
            own = 2 * group + k
            rows = pl.ds(pl.multiple_of((2 * own + (1 - core)) * BLK, BLK), BLK)
            pair_out[own] = encode(gt[rows, :])

    def pair_copy(own):
        return remote(
            pair_out.at[own], pair_in.at[own], pair_s.at[own], pair_r.at[own], dp=partner
        )

    def conv_y_copy(off):
        return remote(
            conv_y.at[y], conv_y.at[y], cy_s.at[off], cy_r.at[y], dp=2 * y_at(off) + core
        )

    turn_group(0)
    conv_load.wait()
    pl.semaphore_wait(barrier, (2 * YS - 1) + (REPS - 1) + (TENS - 1))
    for k in range(2):
        pair_copy(2 * order[0] + k).start()
    for off in range(1, YS):
        conv_y_copy(off).start()
    for i in range(1, 4):
        turn_group(i)
        for k in range(2):
            pair_copy(2 * order[i] + k).start()

    arrived = set()

    def local_sum(off, half):
        own = y_at(off)
        if off % YS not in arrived:
            arrived.add(off % YS)
            pair_copy(own).wait_recv()
        rows = pl.ds(pl.multiple_of((2 * own + core) * BLK + half * HALF, 16), HALF)
        return gt[rows, :] + decode(pair_in[own, half * HALF : half * HALF + HALF, :])

    def ring_copy(first, sign, k):
        return remote(
            ring_out.at[first + k], ring_in.at[first + k], ring_s.at[first + k],
            ring_r.at[first + k], dp=2 * y_at(sign) + core,
        )

    def conv_c_copy():
        return remote(conv_c.at[core], conv_c.at[core], cc_s, cc_r, dp=partner)

    def conv_z_copy(off):
        return remote(
            conv_z.at[rep], conv_z.at[rep], cz_s.at[off], cz_r.at[rep], rep=(rep + off) % REPS
        )

    for k in range(4):
        for first, sign, half, hops in STREAMS:
            if k < hops:
                total = local_sum(sign * (hops - k), half)
                if k:
                    ring_copy(first, sign, k - 1).wait_recv()
                    total = total + decode(ring_in[first + k - 1])
                ring_out[first + k] = encode(total)
                ring_copy(first, sign, k).start()
        if k == 0:
            for off in range(1, YS):
                src = y_at(off)
                remote(conv_y.at[src], conv_y.at[src], cy_s.at[off], cy_r.at[src], dp=partner).wait_recv()
            total = conv_y[0]
            for i in range(1, YS):
                total = total + conv_y[i]
            conv_c[core] = total
            conv_c_copy().start()
        if k == 1:
            conv_c_copy().wait_recv()
            conv_z[rep] = conv_c[0] + conv_c[1]
            for off in range(1, REPS):
                conv_z_copy(off).start()

    halves = []
    for half, (first, sign), (other, other_sign) in ((0, (P0, 1), (M0, -1)), (1, (M1, -1), (P1, 1))):
        total = local_sum(0, half)
        ring_copy(other, other_sign, 2).wait_recv()
        total = total + decode(ring_in[other + 2])
        ring_copy(first, sign, 3).wait_recv()
        total = total + decode(ring_in[first + 3])
        halves.append(total)

    part = (halves[0][0:QUART], halves[0][QUART:], halves[1][0:QUART], halves[1][QUART:])
    for q in range(REPS):
        zq_out[q] = encode(part[q])
        gt[q * QUART : (q + 1) * QUART, :] = part[q]

    def zq_copy(off):
        to = (rep + off) % REPS
        return remote(zq_out.at[to], zq_in.at[rep], zq_s.at[off], zq_r.at[rep], rep=to)

    for off in range(1, REPS):
        zq_copy(off).start()

    for off in range(1, REPS):
        src = (rep + off) % REPS
        remote(conv_z.at[src], conv_z.at[src], cz_s.at[off], cz_r.at[src], dp=partner).wait_recv()
    count = float(REPS * 2 * YS)
    conv_avg = (((conv_z[0] + conv_z[1]) + conv_z[2]) + conv_z[3]) * (1.0 / count)
    conv_square = jnp.sum(conv_avg * conv_avg) * (1.0 / count)

    avg = gt[pl.ds(pl.multiple_of(rep * QUART, 8), QUART), :]
    for off in range(1, REPS):
        src = (rep + off) % REPS
        remote(zq_out.at[src], zq_in.at[src], zq_s.at[off], zq_r.at[src], dp=partner).wait_recv()
        avg = avg + decode(zq_in[src])
    avg = avg * (1.0 / count)
    zg[rep] = encode(avg)

    def zg_copy(off):
        return remote(zg.at[rep], zg.at[rep], zg_s.at[off], zg_r.at[rep], rep=(rep + off) % REPS)

    def spread(buf, send, recv, axis, me, size):
        def start(i, carry):
            to = (me + i) % size
            remote(buf.at[me], buf.at[me], send.at[i], recv.at[me], **{axis: to}).start()
            return carry

        lax.fori_loop(1, size, start, 0)

    def collect(buf, send, recv, axis, me, size):
        def wait(i, carry):
            src = (me + i) % size
            remote(buf.at[src], buf.at[src], send.at[i], recv.at[src], **{axis: src}).wait_recv()
            return carry

        lax.fori_loop(1, size, wait, 0)
        total = buf[0]
        for i in range(1, size):
            total = total + buf[i]
        return total

    def drain(buf, send, recv, axis, me, size):
        def wait(i, carry):
            to = (me + i) % size
            remote(buf.at[me], buf.at[me], send.at[i], recv.at[me], **{axis: to}).wait_send()
            return carry

        lax.fori_loop(1, size, wait, 0)

    norm_r[rep] = fold(avg * avg)
    spread(norm_r, nr_s, nr_r, "rep", rep, REPS)
    for off in range(1, REPS):
        zg_copy(off).start()
    norm_d[dp] = collect(norm_r, nr_s, nr_r, "rep", rep, REPS)
    spread(norm_d, nd_s, nd_r, "dp", dp, 2 * YS)
    norm_t[ten] = collect(norm_d, nd_s, nd_r, "dp", dp, 2 * YS) + conv_square * (float(REPS * 2 * YS) / 1024.0)
    spread(norm_t, nt_s, nt_r, "tensor", ten, TENS)

    for off in range(1, REPS):
        src = (rep + off) % REPS
        remote(zg.at[src], zg.at[src], zg_s.at[off], zg_r.at[src], dp=partner).wait_recv()
    for q in range(REPS):
        gt[q * QUART : (q + 1) * QUART, :] = decode(zg[q])
    for copy in late:
        copy.wait()

    square_sum = jnp.sum(collect(norm_t, nt_s, nt_r, "tensor", ten, TENS), keepdims=True)
    clip = clip_from(square_sum)

    new_param, new_mom, new_vel = adamw_step(p_v[...], m_v[...], v_v[...], clip * gt[0:BLK, :])
    mine = pl.multiple_of(dp * BLK, BLK)
    wt[pl.ds(mine, BLK), :] = new_param.astype(BF16)

    def gather_copy(first, sign, half, k):
        own = y_at(-sign * k)
        rows = pl.ds(pl.multiple_of((2 * own + core) * BLK + half * HALF, 16), HALF)
        return remote(
            wt.at[rows, :], wt.at[rows, :], gather_s.at[first + k], gather_r.at[first + k],
            dp=2 * y_at(sign) + core,
        )

    def share_copy(off, half, whose):
        own = y_at(off)
        at = (2 * own + whose) * BLK + half * HALF
        rows = pl.ds(pl.multiple_of(at, 16), HALF)
        slot = (off % YS) * 2 + half
        return remote(wt.at[rows, :], wt.at[rows, :], share_s.at[slot], share_r.at[slot], dp=partner)

    for first, sign, half, hops in STREAMS:
        gather_copy(first, sign, half, 0).start()
    for half in range(2):
        share_copy(0, half, core).start()

    o_param[...] = new_param
    o_mom[...] = new_mom
    o_vel[...] = new_vel
    new_cparam, new_cmom, new_cvel = adamw_step(cp_v[...], cm_v[...], cv_v[...], clip * conv_avg)
    o_cparam[...] = new_cparam
    o_cmom[...] = new_cmom
    o_cvel[...] = new_cvel

    for k in range(1, 5):
        for first, sign, half, hops in STREAMS:
            if k <= hops:
                gather_copy(first, sign, half, k - 1).wait_recv()
                if k < hops:
                    gather_copy(first, sign, half, k).start()
                share_copy(-sign * k, half, core).start()

    for off in range(YS):
        for half in range(2):
            share_copy(off, half, 1 - core).wait_recv()

    def back(j, carry):
        at = pl.multiple_of(j * 128, 128)
        o_weights[:, pl.ds(at, 128)] = wt[pl.ds(at, 128), :].astype(F32).T.astype(BF16)
        return carry

    lax.fori_loop(0, D // 128, back, 0)
    near = o_weights[pl.ds(pl.multiple_of(y * 2 * EROW, 16), 2 * EROW), :].astype(F32)
    row_block = jnp.where(core == 0, near[0:EROW], near[EROW:])
    o_ema[...] = 0.9 * e_v[...] + 0.1 * row_block

    for off in range(YS):
        pair_copy(y_at(off)).wait_send()
    for first, sign, half, hops in STREAMS:
        for k in range(hops):
            ring_copy(first, sign, k).wait_send()
            gather_copy(first, sign, half, k).wait_send()
    for off in range(YS):
        for half in range(2):
            share_copy(off, half, core).wait_send()
    for off in range(1, YS):
        conv_y_copy(off).wait_send()
    conv_c_copy().wait_send()
    for off in range(1, REPS):
        conv_z_copy(off).wait_send()
        zq_copy(off).wait_send()
        zg_copy(off).wait_send()
    drain(norm_r, nr_s, nr_r, "rep", rep, REPS)
    drain(norm_d, nd_s, nd_r, "dp", dp, 2 * YS)
    drain(norm_t, nt_s, nt_r, "tensor", ten, TENS)


def body(grad_proj, grad_conv, param_proj, m_proj, v_proj, ema_proj, param_conv, m_conv, v_conv):
    small = jax.ShapeDtypeStruct((KCONV, CCOL), F32)
    block = jax.ShapeDtypeStruct((BLK, ROWS), F32)
    dma = pltpu.SemaphoreType.DMA
    outs = pl.pallas_call(
        kernel,
        out_shape=(
            block, block, block,
            jax.ShapeDtypeStruct((EROW, D), F32),
            jax.ShapeDtypeStruct((ROWS, D), BF16),
            small, small, small,
        ),
        in_specs=[pl.BlockSpec(memory_space=pltpu.HBM)] * 9,
        out_specs=[pl.BlockSpec(memory_space=pltpu.VMEM)] * 8,
        scratch_shapes=[
            pltpu.VMEM((ROWS, D), F32),
            pltpu.VMEM((D, ROWS), F32),
            pltpu.VMEM((YS, BLK, ROWS), BF16),
            pltpu.VMEM((YS, BLK, ROWS), BF16),
            pltpu.VMEM((14, HALF, ROWS), BF16),
            pltpu.VMEM((14, HALF, ROWS), BF16),
            pltpu.VMEM((REPS, QUART, ROWS), BF16),
            pltpu.VMEM((REPS, QUART, ROWS), BF16),
            pltpu.VMEM((REPS, QUART, ROWS), BF16),
            pltpu.VMEM((D, ROWS), BF16),
            pltpu.VMEM((BLK, ROWS), F32),
            pltpu.VMEM((BLK, ROWS), F32),
            pltpu.VMEM((BLK, ROWS), F32),
            pltpu.VMEM((EROW, D), F32),
            pltpu.VMEM((YS, KCONV, CCOL), F32),
            pltpu.VMEM((2, KCONV, CCOL), F32),
            pltpu.VMEM((REPS, KCONV, CCOL), F32),
            pltpu.VMEM((KCONV, CCOL), F32),
            pltpu.VMEM((KCONV, CCOL), F32),
            pltpu.VMEM((KCONV, CCOL), F32),
            pltpu.VMEM((REPS, 8, 128), F32),
            pltpu.VMEM((2 * YS, 8, 128), F32),
            pltpu.VMEM((TENS, 8, 128), F32),
            dma((12,)),
            dma((YS,)), dma((YS,)),
            dma((14,)), dma((14,)),
            dma((REPS,)), dma((REPS,)),
            dma((REPS,)), dma((REPS,)),
            dma((14,)), dma((14,)),
            dma((2 * YS,)), dma((2 * YS,)),
            dma((YS,)), dma((YS,)),
            dma, dma,
            dma((REPS,)), dma((REPS,)),
            dma((REPS,)), dma((REPS,)),
            dma((2 * YS,)), dma((2 * YS,)),
            dma((TENS,)), dma((TENS,)),
        ],
        compiler_params=pltpu.CompilerParams(
            collective_id=0, has_side_effects=True, vmem_limit_bytes=48 << 20
        ),
        name="adamw_step",
    )(
        grad_proj[0], grad_conv[0], param_proj.T, m_proj.T, v_proj.T, ema_proj,
        param_conv, m_conv, v_conv,
    )
    new_param, new_m, new_v, new_ema, weights, new_cparam, new_cm, new_cv = outs
    return (new_param.T, new_m.T, new_v.T, new_ema, weights, new_cparam, new_cm, new_cv)


def solution(mesh):
    in_specs = (
        P(("rep", "dp"), "tensor", None),
        P(("rep", "dp"), None, "tensor"),
        P("tensor", "dp"),
        P("tensor", "dp"),
        P("tensor", "dp"),
        P(("tensor", "dp"), None),
        P(None, "tensor"),
        P(None, "tensor"),
        P(None, "tensor"),
    )
    out_specs = (
        P("tensor", "dp"),
        P("tensor", "dp"),
        P("tensor", "dp"),
        P(("tensor", "dp"), None),
        P("tensor", None),
        P(None, "tensor"),
        P(None, "tensor"),
        P(None, "tensor"),
    )
    return jax.shard_map(body, mesh=mesh, in_specs=in_specs, out_specs=out_specs, check_vma=False)
```

```python
import functools
import math

import jax
import jax.numpy as jnp
from jax import lax
from jax.experimental import pallas as pl
from jax.experimental.pallas import tpu as pltpu
from jax.sharding import PartitionSpec as P

D = 1536
INNER = 3072
CONV = 3328
KCONV = 4

F32 = jnp.float32
BF16 = jnp.bfloat16
MESH = pl.DeviceIdType.MESH

YS = 8
REPS = 4
TENS = 8
ROWS = INNER // TENS
BLK = D // (2 * YS)
HALF = BLK // 2
CCOL = CONV // TENS
EROW = ROWS // (2 * YS)
SCALE_UP = 2.0**15
SCALE_DOWN = 2.0**-15


def adamw_step(param_in, first_in, second_in, grad_in):
    first_out = 0.9 * first_in + 0.1 * grad_in
    second_out = 0.95 * second_in + 0.05 * grad_in * grad_in
    bias_one = 1.0 - 0.9**10
    bias_two = 1.0 - 0.95**10
    update = first_out / bias_one / (jnp.sqrt(second_out / bias_two) + 1e-08)
    param_out = param_in - 0.25 * (update + 0.1 * param_in)
    return (param_out, first_out, second_out)


def clip_from(square_sum):
    clip_limit = 0.5 * math.sqrt(INNER * D + KCONV * CONV)
    return jnp.minimum(1.0, clip_limit / (jnp.sqrt(square_sum) + 1e-06))


def encode(x):
    wide = x * SCALE_UP
    square = wide * wide
    return ((square * wide) * jnp.abs(wide)).astype(BF16)


def signed_root(x):
    return x * lax.rsqrt(jnp.maximum(jnp.abs(x), 1e-37))


def decode(code):
    return signed_root(signed_root(code.astype(F32))) * SCALE_DOWN


def fold(x):
    total = x[0:8, 0:128]
    for i in range(x.shape[0] // 8):
        for j in range(x.shape[1] // 128):
            if i or j:
                total = total + x[8 * i : 8 * i + 8, 128 * j : 128 * j + 128]
    return total


WAYS = ((1, 0), (-1, 1))


def kernel(
    grad, conv, param, mom, vel, ema, cparam, cmom, cvel,
    o_param, o_mom, o_vel, o_ema, o_weights, o_cparam, o_cmom, o_cvel,
    g_in, gt, pair_out, pair_in, far_out, far_in, mid_out, mid_in, rel_out, rel_in, near_out, near_in,
    zx, wt, p_v, m_v, v_v, e_v, conv_y, conv_c, conv_z, cp_v, cm_v, cv_v, norm_d, norm_t,
    load_sem, pair_s, pair_r, far_s, far_r, mid_s, mid_r, rel_s, rel_r, near_s, near_r, zx_s, zx_r,
    own_s, own_r, fwd_s, fwd_r, share_s, share_r, cy_s, cy_r, cc_s, cc_r, cz_s, cz_r,
    nd_s, nd_r, nt_s, nt_r,
):
    rep = lax.axis_index("rep")
    dp = lax.axis_index("dp")
    ten = lax.axis_index("tensor")
    y = dp // 2
    core = dp % 2
    partner = 2 * y + (1 - core)

    def y_at(off):
        return (y + (off + YS)) % YS

    def remote(src, dst, send, recv, **device):
        return pltpu.make_async_remote_copy(
            src_ref=src, dst_ref=dst, send_sem=send, recv_sem=recv,
            device_id=device, device_id_type=MESH,
        )

    base = (y // 2 + 2) % 4
    turn = 2 * (y % 2) - 1
    order = (base, (base + turn + 4) % 4, (base - turn + 4) % 4, (base + 2) % 4)
    loads = []
    for i, group in enumerate(order):
        cols = pl.ds(pl.multiple_of(group * 384, 128), 384)
        loads.append(pltpu.make_async_copy(grad.at[:, cols], g_in.at[:, cols], load_sem.at[i]))
        loads[-1].start()
    conv_load = pltpu.make_async_copy(conv, conv_y.at[y], load_sem.at[4])
    conv_load.start()
    late = []
    for i, (src, dst) in enumerate(
        ((param, p_v), (mom, m_v), (vel, v_v), (ema, e_v), (cparam, cp_v), (cmom, cm_v), (cvel, cv_v))
    ):
        late.append(pltpu.make_async_copy(src, dst, load_sem.at[5 + i]))
        late[-1].start()

    barrier = pltpu.get_barrier_semaphore()

    def greet(axis, me, count):
        def step(i, carry):
            pl.semaphore_signal(
                barrier, inc=1, device_id={axis: (me + i) % count}, device_id_type=MESH
            )
            return carry

        lax.fori_loop(1, count, step, 0)

    greet("dp", dp, 2 * YS)
    greet("rep", rep, REPS)
    greet("tensor", ten, TENS)

    def turn_group(i):
        loads[i].wait()
        group = order[i]

        def step(j, carry):
            at = pl.multiple_of(group * 384 + j * 128, 128)
            gt[pl.ds(at, 128), :] = g_in[:, pl.ds(at, 128)].T
            return carry

        lax.fori_loop(0, 3, step, 0)
        for k in range(2):
            own = 2 * group + k
            rows = pl.ds(pl.multiple_of((2 * own + (1 - core)) * BLK, BLK), BLK)
            pair_out[own] = encode(gt[rows, :])

    def pair_copy(own):
        return remote(
            pair_out.at[own], pair_in.at[own], pair_s.at[own], pair_r.at[own], dp=partner
        )

    def conv_y_copy(off):
        return remote(
            conv_y.at[y], conv_y.at[y], cy_s.at[off], cy_r.at[y], dp=2 * y_at(off) + core
        )

    turn_group(0)
    conv_load.wait()
    pl.semaphore_wait(barrier, (2 * YS - 1) + (REPS - 1) + (TENS - 1))
    for k in range(2):
        pair_copy(2 * order[0] + k).start()
    for off in range(1, YS):
        conv_y_copy(off).start()
    for i in range(1, 4):
        turn_group(i)
        for k in range(2):
            pair_copy(2 * order[i] + k).start()

    arrived = set()

    def local_sum(off, half=None):
        own = y_at(off)
        if off % YS not in arrived:
            arrived.add(off % YS)
            pair_copy(own).wait_recv()
        lo, n = (0, BLK) if half is None else (half * HALF, HALF)
        rows = pl.ds(pl.multiple_of((2 * own + core) * BLK + lo, 16), n)
        return gt[rows, :] + decode(pair_in[own, lo : lo + n, :])

    def y_copy(out, into, send, recv, i, hops):
        return remote(out.at[i], into.at[i], send.at[i], recv.at[i], dp=2 * y_at(hops) + core)

    def far_copy(i):
        return y_copy(far_out, far_in, far_s, far_r, i, 2 * WAYS[i][0])

    def mid_copy(i):
        return y_copy(mid_out, mid_in, mid_s, mid_r, i, WAYS[i][0])

    def rel_copy(i, half):
        return y_copy(rel_out, rel_in, rel_s, rel_r, 2 * i + half, 2 * WAYS[i][0])

    def near_copy(i):
        return y_copy(near_out, near_in, near_s, near_r, i, WAYS[i][0])

    def conv_c_copy():
        return remote(conv_c.at[core], conv_c.at[core], cc_s, cc_r, dp=partner)

    def conv_z_copy(off):
        return remote(
            conv_z.at[rep], conv_z.at[rep], cz_s.at[off], cz_r.at[rep], rep=(rep + off) % REPS
        )

    for i, (sign, half) in enumerate(WAYS):
        far_out[i] = encode(local_sum(4 * sign, half))
        far_copy(i).start()
    for i, (sign, _) in enumerate(WAYS):
        mid_out[i] = encode(local_sum(3 * sign))
        mid_copy(i).start()
    for i, (sign, _) in enumerate(WAYS):
        near_out[i] = encode(local_sum(sign))
        near_copy(i).start()

    for off in range(1, YS):
        src = y_at(off)
        remote(conv_y.at[src], conv_y.at[src], cy_s.at[off], cy_r.at[src], dp=partner).wait_recv()
    total = conv_y[0]
    for i in range(1, YS):
        total = total + conv_y[i]
    conv_c[core] = total
    conv_c_copy().start()
    for i, (sign, half) in enumerate(WAYS):
        mid_copy(i).wait_recv()
        far_copy(i).wait_recv()
        for h in (half, 1 - half):
            total = local_sum(2 * sign, h) + decode(mid_in[i, h * HALF : (h + 1) * HALF, :])
            if h == half:
                total = total + decode(far_in[i])
            rel_out[2 * i + h] = encode(total)
            rel_copy(i, h).start()
    conv_c_copy().wait_recv()
    conv_z[rep] = conv_c[0] + conv_c[1]
    for off in range(1, REPS):
        conv_z_copy(off).start()

    mine_sum = [local_sum(0, h) for h in range(2)]
    for i in range(2):
        near_copy(i).wait_recv()
        for h in range(2):
            mine_sum[h] = mine_sum[h] + decode(near_in[i, h * HALF : (h + 1) * HALF, :])

    def zx_copy(off, h):
        return remote(
            zx.at[2 * rep + h], zx.at[2 * rep + h], zx_s.at[2 * off + h], zx_r.at[2 * rep + h],
            rep=(rep + off) % REPS,
        )

    for h in range(2):
        for i in range(2):
            rel_copy(i, h).wait_recv()
            mine_sum[h] = mine_sum[h] + decode(rel_in[2 * i + h])
        zx[2 * rep + h] = encode(mine_sum[h])
        for off in (2, 1, 3):
            zx_copy(off, h).start()

    for off in range(1, REPS):
        src = (rep + off) % REPS
        remote(conv_z.at[src], conv_z.at[src], cz_s.at[off], cz_r.at[src], dp=partner).wait_recv()
    count = float(REPS * 2 * YS)
    conv_avg = (((conv_z[0] + conv_z[1]) + conv_z[2]) + conv_z[3]) * (1.0 / count)
    conv_square = jnp.sum(conv_avg * conv_avg)

    avg = []
    for h in range(2):
        for off in range(1, REPS):
            src = 2 * ((rep + off) % REPS) + h
            remote(zx.at[src], zx.at[src], zx_s.at[2 * off + h], zx_r.at[src], dp=partner).wait_recv()
        total = decode(zx[h])
        for r in range(1, REPS):
            total = total + decode(zx[2 * r + h])
        avg.append(total * (1.0 / count))

    def row_copy(buf, send, recv, axis, me, i, size):
        to = (me + i) % size
        at = buf.at[me, pl.ds(0, 1), :]
        return remote(at, at, send.at[i], recv.at[me], **{axis: to})

    def spread(buf, send, recv, axis, me, size):
        def start(i, carry):
            row_copy(buf, send, recv, axis, me, i, size).start()
            return carry

        lax.fori_loop(1, size, start, 0)

    def collect(buf, send, recv, axis, me, size):
        def wait(i, carry):
            src = (me + i) % size
            at = buf.at[src, pl.ds(0, 1), :]
            remote(at, at, send.at[i], recv.at[src], **{axis: src}).wait_recv()
            return carry

        lax.fori_loop(1, size, wait, 0)
        total = buf[0, 0:1, :]
        for i in range(1, size):
            total = total + buf[i, 0:1, :]
        return total

    def drain(buf, send, recv, axis, me, size):
        def wait(i, carry):
            row_copy(buf, send, recv, axis, me, i, size).wait_send()
            return carry

        lax.fori_loop(1, size, wait, 0)

    square = fold(avg[0] * avg[0]) + fold(avg[1] * avg[1])
    norm_d[dp, 0:1, :] = jnp.sum(square, axis=0, keepdims=True)
    spread(norm_d, nd_s, nd_r, "dp", dp, 2 * YS)
    for h in range(2):
        gt[h * HALF : (h + 1) * HALF, :] = avg[h]
    for copy in late:
        copy.wait()
    norm_t[ten, 0:1, :] = collect(norm_d, nd_s, nd_r, "dp", dp, 2 * YS) + conv_square * (1.0 / 128.0)
    spread(norm_t, nt_s, nt_r, "tensor", ten, TENS)

    square_sum = jnp.sum(collect(norm_t, nt_s, nt_r, "tensor", ten, TENS), keepdims=True)
    clip = clip_from(square_sum)

    new_param, new_mom, new_vel = adamw_step(p_v[...], m_v[...], v_v[...], clip * gt[0:BLK, :])
    mine = pl.multiple_of(dp * BLK, BLK)
    wt[pl.ds(mine, BLK), :] = new_param.astype(BF16)

    def rows_of(off, whose, half=None):
        lo, n = (0, BLK) if half is None else (half * HALF, HALF)
        return pl.ds(pl.multiple_of((2 * y_at(off) + whose) * BLK + lo, 16), n)

    def gather_copy(send, recv, slot, off, half, hops):
        rows = rows_of(off, core, half)
        return remote(
            wt.at[rows, :], wt.at[rows, :], send.at[slot], recv.at[slot], dp=2 * y_at(hops) + core
        )

    def own2_copy(i, half):
        return gather_copy(own_s, own_r, 2 * i + half, 0, half, 2 * WAYS[i][0])

    def own1_copy(i):
        return gather_copy(own_s, own_r, 4 + i, 0, None, WAYS[i][0])

    def fwd1_copy(i, half):
        return gather_copy(fwd_s, fwd_r, 2 * i + half, -2 * WAYS[i][0], half, WAYS[i][0])

    def fwd2_copy(i):
        sign, half = WAYS[i]
        return gather_copy(fwd_s, fwd_r, 4 + i, -2 * sign, half, 2 * sign)

    def share_copy(off, half, whose):
        rows = rows_of(off, whose, half)
        slot = 2 * y_at(off) + (half or 0)
        return remote(wt.at[rows, :], wt.at[rows, :], share_s.at[slot], share_r.at[slot], dp=partner)

    for k in range(2):
        for i, (sign, half) in enumerate(WAYS):
            own2_copy(i, half if k == 0 else 1 - half).start()
    for i in range(2):
        own1_copy(i).start()
    share_copy(0, None, core).start()

    o_param[...] = new_param
    o_mom[...] = new_mom
    o_vel[...] = new_vel
    new_cparam, new_cmom, new_cvel = adamw_step(cp_v[...], cm_v[...], cv_v[...], clip * conv_avg)
    o_cparam[...] = new_cparam
    o_cmom[...] = new_cmom
    o_cvel[...] = new_cvel

    for k in range(2):
        for i, (sign, half) in enumerate(WAYS):
            h = half if k == 0 else 1 - half
            own2_copy(i, h).wait_recv()
            if k == 0:
                fwd2_copy(i).start()
            fwd1_copy(i, h).start()
            share_copy(-2 * sign, h, core).start()
    for i, (sign, _) in enumerate(WAYS):
        own1_copy(i).wait_recv()
        share_copy(-sign, None, core).start()

    def back(first):
        def step(j, carry):
            at = pl.multiple_of(first * 192 + j * 128, 128)
            o_weights[:, pl.ds(at, 128)] = wt[pl.ds(at, 128), :].astype(F32).T.astype(BF16)
            return carry

        lax.fori_loop(0, 3, step, 0)

    share_copy(0, None, 1 - core).wait_recv()
    for sign, _ in WAYS:
        share_copy(-sign, None, 1 - core).wait_recv()
        for h in range(2):
            share_copy(-2 * sign, h, 1 - core).wait_recv()
    pair = y // 2
    back(2 * pair)
    back(2 * ((pair + turn + 4) % 4))
    for i, (sign, half) in enumerate(WAYS):
        fwd2_copy(i).wait_recv()
        share_copy(-4 * sign, half, core).start()
    for k in range(2):
        for i, (sign, half) in enumerate(WAYS):
            h = half if k == 0 else 1 - half
            fwd1_copy(i, h).wait_recv()
            share_copy(-3 * sign, h, core).start()
    for off in (4, 3, -3):
        for h in range(2):
            share_copy(off, h, 1 - core).wait_recv()
    back(2 * ((pair - turn + 4) % 4))
    back(2 * ((pair + 2) % 4))
    near = o_weights[pl.ds(pl.multiple_of(y * 2 * EROW, 16), 2 * EROW), :].astype(F32)
    row_block = jnp.where(core == 0, near[0:EROW], near[EROW:])
    o_ema[...] = 0.9 * e_v[...] + 0.1 * row_block

    for off in range(YS):
        pair_copy(y_at(off)).wait_send()
    for i, (sign, half) in enumerate(WAYS):
        far_copy(i).wait_send()
        mid_copy(i).wait_send()
        near_copy(i).wait_send()
        own1_copy(i).wait_send()
        fwd2_copy(i).wait_send()
        share_copy(-sign, None, core).wait_send()
        share_copy(-4 * sign, half, core).wait_send()
        for h in range(2):
            rel_copy(i, h).wait_send()
            own2_copy(i, h).wait_send()
            fwd1_copy(i, h).wait_send()
            share_copy(-2 * sign, h, core).wait_send()
            share_copy(-3 * sign, h, core).wait_send()
    share_copy(0, None, core).wait_send()
    for off in range(1, YS):
        conv_y_copy(off).wait_send()
    conv_c_copy().wait_send()
    for off in range(1, REPS):
        conv_z_copy(off).wait_send()
        for h in range(2):
            zx_copy(off, h).wait_send()
    drain(norm_d, nd_s, nd_r, "dp", dp, 2 * YS)
    drain(norm_t, nt_s, nt_r, "tensor", ten, TENS)


def hand_over(*refs):
    sems = refs[-1]
    copies = [
        pltpu.make_async_copy(refs[i], refs[8 + i], sems.at[i]) for i in (4, 0, 1, 2, 3, 5, 6, 7)
    ]
    for copy in copies:
        copy.start()
    for copy in copies:
        copy.wait()


def body(grad_proj, grad_conv, param_proj, m_proj, v_proj, ema_proj, param_conv, m_conv, v_conv):
    small = jax.ShapeDtypeStruct((KCONV, CCOL), F32)
    block = jax.ShapeDtypeStruct((BLK, ROWS), F32)
    dma = pltpu.SemaphoreType.DMA
    outs = pl.pallas_call(
        kernel,
        out_shape=(
            block, block, block,
            jax.ShapeDtypeStruct((EROW, D), F32),
            jax.ShapeDtypeStruct((ROWS, D), BF16),
            small, small, small,
        ),
        in_specs=[pl.BlockSpec(memory_space=pltpu.HBM)] * 9,
        out_specs=[pl.BlockSpec(memory_space=pltpu.VMEM)] * 8,
        scratch_shapes=[
            pltpu.VMEM((ROWS, D), F32),
            pltpu.VMEM((D, ROWS), F32),
            pltpu.VMEM((YS, BLK, ROWS), BF16),
            pltpu.VMEM((YS, BLK, ROWS), BF16),
            pltpu.VMEM((2, HALF, ROWS), BF16),
            pltpu.VMEM((2, HALF, ROWS), BF16),
            pltpu.VMEM((2, BLK, ROWS), BF16),
            pltpu.VMEM((2, BLK, ROWS), BF16),
            pltpu.VMEM((4, HALF, ROWS), BF16),
            pltpu.VMEM((4, HALF, ROWS), BF16),
            pltpu.VMEM((2, BLK, ROWS), BF16),
            pltpu.VMEM((2, BLK, ROWS), BF16),
            pltpu.VMEM((2 * REPS, HALF, ROWS), BF16),
            pltpu.VMEM((D, ROWS), BF16),
            pltpu.VMEM((BLK, ROWS), F32),
            pltpu.VMEM((BLK, ROWS), F32),
            pltpu.VMEM((BLK, ROWS), F32),
            pltpu.VMEM((EROW, D), F32),
            pltpu.VMEM((YS, KCONV, CCOL), F32),
            pltpu.VMEM((2, KCONV, CCOL), F32),
            pltpu.VMEM((REPS, KCONV, CCOL), F32),
            pltpu.VMEM((KCONV, CCOL), F32),
            pltpu.VMEM((KCONV, CCOL), F32),
            pltpu.VMEM((KCONV, CCOL), F32),
            pltpu.VMEM((2 * YS, 8, 128), F32),
            pltpu.VMEM((TENS, 8, 128), F32),
            dma((12,)),
            dma((YS,)), dma((YS,)),
            dma((2,)), dma((2,)),
            dma((2,)), dma((2,)),
            dma((4,)), dma((4,)),
            dma((2,)), dma((2,)),
            dma((2 * REPS,)), dma((2 * REPS,)),
            dma((6,)), dma((6,)),
            dma((6,)), dma((6,)),
            dma((2 * YS,)), dma((2 * YS,)),
            dma((YS,)), dma((YS,)),
            dma, dma,
            dma((REPS,)), dma((REPS,)),
            dma((2 * YS,)), dma((2 * YS,)),
            dma((TENS,)), dma((TENS,)),
        ],
        compiler_params=pltpu.CompilerParams(
            collective_id=0, has_side_effects=True, vmem_limit_bytes=48 << 20
        ),
        name="adamw_step",
    )(
        *(
            pltpu.with_memory_space_constraint(x, pltpu.HBM)
            for x in (
                grad_proj[0], grad_conv[0], param_proj.T, m_proj.T, v_proj.T, ema_proj,
                param_conv, m_conv, v_conv,
            )
        )
    )
    outs = pl.pallas_call(
        hand_over,
        out_shape=tuple(jax.ShapeDtypeStruct(x.shape, x.dtype) for x in outs),
        in_specs=[pl.BlockSpec(memory_space=pltpu.VMEM)] * 8,
        out_specs=[pl.BlockSpec(memory_space=pltpu.HBM)] * 8,
        scratch_shapes=[dma((8,))],
        name="hand_over",
    )(*(pltpu.with_memory_space_constraint(x, pltpu.VMEM) for x in outs))
    new_param, new_m, new_v, new_ema, weights, new_cparam, new_cm, new_cv = outs
    return (new_param.T, new_m.T, new_v.T, new_ema, weights, new_cparam, new_cm, new_cv)


def solution(mesh):
    in_specs = (
        P(("rep", "dp"), "tensor", None),
        P(("rep", "dp"), None, "tensor"),
        P("tensor", "dp"),
        P("tensor", "dp"),
        P("tensor", "dp"),
        P(("tensor", "dp"), None),
        P(None, "tensor"),
        P(None, "tensor"),
        P(None, "tensor"),
    )
    out_specs = (
        P("tensor", "dp"),
        P("tensor", "dp"),
        P("tensor", "dp"),
        P(("tensor", "dp"), None),
        P("tensor", None),
        P(None, "tensor"),
        P(None, "tensor"),
        P(None, "tensor"),
    )
    return jax.shard_map(body, mesh=mesh, in_specs=in_specs, out_specs=out_specs, check_vma=False)
```

```python
import functools
import math

import jax
import jax.numpy as jnp
from jax import lax
from jax.experimental import pallas as pl
from jax.experimental.pallas import tpu as pltpu
from jax.sharding import PartitionSpec as P

D = 1536
INNER = 3072
CONV = 3328
KCONV = 4

F32 = jnp.float32
BF16 = jnp.bfloat16
MESH = pl.DeviceIdType.MESH

YS = 8
REPS = 4
TENS = 8
ROWS = INNER // TENS
BLK = D // (2 * YS)
HALF = BLK // 2
CCOL = CONV // TENS
EROW = ROWS // (2 * YS)
SCALE_UP = 2.0**15
SCALE_DOWN = 2.0**-15


def adamw_step(param_in, first_in, second_in, grad_in):
    first_out = 0.9 * first_in + 0.1 * grad_in
    second_out = 0.95 * second_in + 0.05 * grad_in * grad_in
    bias_one = 1.0 - 0.9**10
    bias_two = 1.0 - 0.95**10
    update = first_out / bias_one / (jnp.sqrt(second_out / bias_two) + 1e-08)
    param_out = param_in - 0.25 * (update + 0.1 * param_in)
    return (param_out, first_out, second_out)


def clip_from(square_sum):
    clip_limit = 0.5 * math.sqrt(INNER * D + KCONV * CONV)
    return jnp.minimum(1.0, clip_limit / (jnp.sqrt(square_sum) + 1e-06))


def encode(x):
    wide = x * SCALE_UP
    square = wide * wide
    return ((square * wide) * jnp.abs(wide)).astype(BF16)


def signed_root(x):
    return x * lax.rsqrt(jnp.maximum(jnp.abs(x), 1e-37))


def decode(code):
    return signed_root(signed_root(code.astype(F32))) * SCALE_DOWN


def fold(x):
    total = x[0:8, 0:128]
    for i in range(x.shape[0] // 8):
        for j in range(x.shape[1] // 128):
            if i or j:
                total = total + x[8 * i : 8 * i + 8, 128 * j : 128 * j + 128]
    return total


WAYS = ((1, 0), (-1, 1))


def kernel(
    grad, conv, param, mom, vel, ema, cparam, cmom, cvel,
    o_param, o_mom, o_vel, o_ema, o_weights, o_cparam, o_cmom, o_cvel,
    g_in, gt, pair_out, pair_in, far_out, far_in, mid_out, mid_in, rel_out, rel_in, near_out, near_in,
    zx, wt, p_v, m_v, v_v, e_v, conv_y, conv_c, conv_z, cp_v, cm_v, cv_v, norm_d, norm_t,
    load_sem, pair_s, pair_r, far_s, far_r, mid_s, mid_r, rel_s, rel_r, near_s, near_r, zx_s, zx_r,
    own_s, own_r, fwd_s, fwd_r, share_s, share_r, cy_s, cy_r, cc_s, cc_r, cz_s, cz_r,
    nd_s, nd_r, nt_s, nt_r, hello_z, hello_x,
):
    rep = lax.axis_index("rep")
    dp = lax.axis_index("dp")
    ten = lax.axis_index("tensor")
    y = dp // 2
    core = dp % 2
    partner = 2 * y + (1 - core)

    def y_at(off):
        return (y + off + YS) % YS

    def remote(src, dst, send, recv, **device):
        return pltpu.make_async_remote_copy(
            src_ref=src, dst_ref=dst, send_sem=send, recv_sem=recv,
            device_id=device, device_id_type=MESH,
        )

    base = (y // 2 + 2) % 4
    turn = 2 * (y % 2) - 1
    order = (base, (base + turn + 4) % 4, (base - turn + 4) % 4, (base + 2) % 4)
    loads = []
    for i, group in enumerate(order):
        cols = pl.ds(pl.multiple_of(group * 384, 128), 384)
        loads.append(pltpu.make_async_copy(grad.at[:, cols], g_in.at[:, cols], load_sem.at[i]))
    for copy in loads:
        copy.start()
    conv_load = pltpu.make_async_copy(conv, conv_z.at[rep], load_sem.at[4])
    late = []
    for i, (src, dst) in enumerate(
        ((param, p_v), (mom, m_v), (vel, v_v), (ema, e_v), (cparam, cp_v), (cmom, cm_v), (cvel, cv_v))
    ):
        late.append(pltpu.make_async_copy(src, dst, load_sem.at[5 + i]))

    x_near = [{"tensor": (ten + 2) % TENS}, {"tensor": (ten + TENS - 2) % TENS}, {"tensor": ten + 1 - 2 * (ten % 2)}]
    z_near = [{"rep": (rep + 1) % REPS}, {"rep": (rep + REPS - 1) % REPS}]
    y_near = [{"dp": 2 * y_at(off) + core} for off in (2, -2, 1, -1)]
    barrier = pltpu.get_barrier_semaphore()

    def signal(sem, devices):
        for device in devices:
            pl.semaphore_signal(sem, inc=1, device_id=device, device_id_type=MESH)

    signal(barrier, y_near[:2] + z_near + y_near[2:] + x_near + [{"dp": partner}])

    def turn_group(i):
        loads[i].wait()
        group = order[i]

        def step(j, carry):
            at = pl.multiple_of(group * 384 + j * 128, 128)
            gt[pl.ds(at, 128), :] = g_in[:, pl.ds(at, 128)].T
            return carry

        lax.fori_loop(0, 3, step, 0)
        for k in range(2):
            own = 2 * group + k
            rows = pl.ds(pl.multiple_of((2 * own + (1 - core)) * BLK, BLK), BLK)
            pair_out[own] = encode(gt[rows, :])

    def pair_copy(own):
        return remote(
            pair_out.at[own], pair_in.at[own], pair_s.at[own], pair_r.at[own], dp=partner
        )

    def conv_y_copy(off):
        return remote(
            conv_y.at[y], conv_y.at[y], cy_s.at[off], cy_r.at[y], dp=2 * y_at(off) + core
        )

    for copy in [conv_load] + late:
        copy.start()
    for i in range(4):
        turn_group(i)
    pl.semaphore_wait(barrier, 10)
    for i in range(4):
        for k in range(2):
            pair_copy(2 * order[i] + k).start()
    signal(hello_z, z_near)
    signal(hello_x.at[0], x_near)

    arrived = set()

    def local_sum(off, half=None):
        own = y_at(off)
        if off % YS not in arrived:
            arrived.add(off % YS)
            pair_copy(own).wait_recv()
        lo, n = (0, BLK) if half is None else (half * HALF, HALF)
        rows = pl.ds(pl.multiple_of((2 * own + core) * BLK + lo, 16), n)
        return gt[rows, :] + decode(pair_in[own, lo : lo + n, :])

    def y_copy(out, into, send, recv, i, hops):
        return remote(out.at[i], into.at[i], send.at[i], recv.at[i], dp=2 * y_at(hops) + core)

    def far_copy(i):
        return y_copy(far_out, far_in, far_s, far_r, i, 2 * WAYS[i][0])

    def mid_copy(i, half):
        return y_copy(mid_out, mid_in, mid_s, mid_r, 2 * i + half, WAYS[i][0])

    def rel_copy(i, half):
        return y_copy(rel_out, rel_in, rel_s, rel_r, 2 * i + half, 2 * WAYS[i][0])

    def near_copy(i, half):
        return y_copy(near_out, near_in, near_s, near_r, 2 * i + half, WAYS[i][0])

    def conv_c_copy():
        return remote(conv_c.at[core], conv_c.at[core], cc_s, cc_r, dp=partner)

    def conv_z_copy(off):
        return remote(
            conv_z.at[rep], conv_z.at[rep], cz_s.at[off], cz_r.at[rep], rep=(rep + off) % REPS
        )

    for i, (sign, half) in enumerate(WAYS):
        far_out[i] = encode(local_sum(4 * sign, half))
        far_copy(i).start()
    for h in range(2):
        for i, (sign, _) in enumerate(WAYS):
            mid_out[2 * i + h] = encode(local_sum(3 * sign, h))
            mid_copy(i, h).start()
    for h in range(2):
        for i, (sign, _) in enumerate(WAYS):
            near_out[2 * i + h] = encode(local_sum(sign, h))
    for i in range(2):
        mid_copy(i, 1).wait_send()
    for h in range(2):
        for i in range(2):
            near_copy(i, h).start()
    for i, h in ((0, 0), (1, 0), (1, 1), (0, 1)):
        mid_copy(i, h).wait_recv()
        total = local_sum(2 * WAYS[i][0], h) + decode(mid_in[2 * i + h])
        if h == WAYS[i][1]:
            far_copy(i).wait_recv()
            total = total + decode(far_in[i])
        rel_out[2 * i + h] = encode(total)
        rel_copy(i, h).start()
    conv_load.wait()
    pl.semaphore_wait(hello_z, 2)
    for off in range(1, REPS):
        conv_z_copy(off).start()
    pl.semaphore_wait(hello_x.at[0], 3)
    signal(hello_x.at[1], x_near)

    def zx_copy(off, h):
        return remote(
            zx.at[2 * rep + h], zx.at[2 * rep + h], zx_s.at[2 * off + h], zx_r.at[2 * rep + h],
            rep=(rep + off) % REPS,
        )

    for h in range(2):
        total = local_sum(0, h)
        for i in range(2):
            near_copy(i, h).wait_recv()
            total = total + decode(near_in[2 * i + h])
        for i in range(2):
            rel_copy(i, h).wait_recv()
            total = total + decode(rel_in[2 * i + h])
        zx[2 * rep + h] = encode(total)
        for off in (2, 1, 3):
            zx_copy(off, h).start()

    count = float(REPS * 2 * YS)
    for off in range(1, REPS):
        src = (rep + off) % REPS
        remote(conv_z.at[src], conv_z.at[src], cz_s.at[off], cz_r.at[src], dp=partner).wait_recv()
    conv_y[y] = ((conv_z[0] + conv_z[1]) + conv_z[2]) + conv_z[3]
    for off in range(1, YS):
        conv_y_copy(off).start()

    avg = []
    for h in range(2):
        for off in range(1, REPS):
            src = 2 * ((rep + off) % REPS) + h
            remote(zx.at[src], zx.at[src], zx_s.at[2 * off + h], zx_r.at[src], dp=partner).wait_recv()
        total = decode(zx[h])
        for r in range(1, REPS):
            total = total + decode(zx[2 * r + h])
        avg.append(total * (1.0 / count))
        if h == 0:
            for off in range(1, YS):
                src = y_at(off)
                remote(conv_y.at[src], conv_y.at[src], cy_s.at[off], cy_r.at[src], dp=partner).wait_recv()
            total = conv_y[0]
            for i in range(1, YS):
                total = total + conv_y[i]
            conv_c[core] = total
            conv_c_copy().start()

    def row_copy(buf, send, recv, axis, me, i, size):
        to = (me + i) % size
        at = buf.at[me, pl.ds(0, 1), :]
        return remote(at, at, send.at[i], recv.at[me], **{axis: to})

    def spread(buf, send, recv, axis, me, size):
        def start(i, carry):
            row_copy(buf, send, recv, axis, me, i, size).start()
            return carry

        lax.fori_loop(1, size, start, 0)

    def collect(buf, send, recv, axis, me, size):
        def wait(i, carry):
            src = (me + i) % size
            at = buf.at[src, pl.ds(0, 1), :]
            remote(at, at, send.at[i], recv.at[src], **{axis: src}).wait_recv()
            return carry

        lax.fori_loop(1, size, wait, 0)
        total = buf[0, 0:1, :]
        for i in range(1, size):
            total = total + buf[i, 0:1, :]
        return total

    def drain(buf, send, recv, axis, me, size):
        def wait(i, carry):
            row_copy(buf, send, recv, axis, me, i, size).wait_send()
            return carry

        lax.fori_loop(1, size, wait, 0)

    square = fold(avg[0] * avg[0]) + fold(avg[1] * avg[1])
    norm_d[dp, 0:1, :] = jnp.sum(square, axis=0, keepdims=True)
    spread(norm_d, nd_s, nd_r, "dp", dp, 2 * YS)
    for h in range(2):
        gt[h * HALF : (h + 1) * HALF, :] = avg[h]
    for copy in late:
        copy.wait()
    conv_c_copy().wait_recv()
    conv_avg = (conv_c[0] + conv_c[1]) * (1.0 / count)
    conv_square = jnp.sum(conv_avg * conv_avg)
    pl.semaphore_wait(hello_x.at[1], 3)
    norm_t[ten, 0:1, :] = collect(norm_d, nd_s, nd_r, "dp", dp, 2 * YS) + conv_square * (1.0 / 128.0)
    spread(norm_t, nt_s, nt_r, "tensor", ten, TENS)

    square_sum = jnp.sum(collect(norm_t, nt_s, nt_r, "tensor", ten, TENS), keepdims=True)
    clip = clip_from(square_sum)

    new_param, new_mom, new_vel = adamw_step(p_v[...], m_v[...], v_v[...], clip * gt[0:BLK, :])
    mine = pl.multiple_of(dp * BLK, BLK)
    wt[pl.ds(mine, BLK), :] = new_param.astype(BF16)

    def rows_of(off, whose, half=None):
        lo, n = (0, BLK) if half is None else (half * HALF, HALF)
        return pl.ds(pl.multiple_of((2 * y_at(off) + whose) * BLK + lo, 16), n)

    def gather_copy(send, recv, slot, off, half, hops):
        rows = rows_of(off, core, half)
        return remote(
            wt.at[rows, :], wt.at[rows, :], send.at[slot], recv.at[slot], dp=2 * y_at(hops) + core
        )

    def own2_copy(i, half):
        return gather_copy(own_s, own_r, 2 * i + half, 0, half, 2 * WAYS[i][0])

    def own1_copy(i):
        return gather_copy(own_s, own_r, 4 + i, 0, None, WAYS[i][0])

    def fwd1_copy(i, half):
        return gather_copy(fwd_s, fwd_r, 2 * i + half, -2 * WAYS[i][0], half, WAYS[i][0])

    def fwd2_copy(i):
        sign, half = WAYS[i]
        return gather_copy(fwd_s, fwd_r, 4 + i, -2 * sign, half, 2 * sign)

    def share_copy(off, half, whose):
        rows = rows_of(off, whose, half)
        slot = 2 * y_at(off) + (half or 0)
        return remote(wt.at[rows, :], wt.at[rows, :], share_s.at[slot], share_r.at[slot], dp=partner)

    for k in range(2):
        for i, (sign, half) in enumerate(WAYS):
            own2_copy(i, half if k == 0 else 1 - half).start()
    share_copy(0, None, core).start()

    o_param[...] = new_param
    o_mom[...] = new_mom
    o_vel[...] = new_vel
    new_cparam, new_cmom, new_cvel = adamw_step(cp_v[...], cm_v[...], cv_v[...], clip * conv_avg)
    o_cparam[...] = new_cparam
    o_cmom[...] = new_cmom
    o_cvel[...] = new_cvel

    for h in range(2):
        for i in range(2):
            own2_copy(i, h).wait_send()
    for i in range(2):
        own1_copy(i).start()

    for off in range(YS):
        pair_copy(y_at(off)).wait_send()
    for i in range(2):
        far_copy(i).wait_send()
        mid_copy(i, 0).wait_send()
        for h in range(2):
            near_copy(i, h).wait_send()
            rel_copy(i, h).wait_send()
    for off in range(1, YS):
        conv_y_copy(off).wait_send()
    conv_c_copy().wait_send()
    for off in range(1, REPS):
        conv_z_copy(off).wait_send()
        for h in range(2):
            zx_copy(off, h).wait_send()
    drain(norm_d, nd_s, nd_r, "dp", dp, 2 * YS)
    drain(norm_t, nt_s, nt_r, "tensor", ten, TENS)

    for k in range(2):
        for i, (sign, half) in enumerate(WAYS):
            h = half if k == 0 else 1 - half
            own2_copy(i, h).wait_recv()
            if k == 0:
                fwd2_copy(i).start()
            fwd1_copy(i, h).start()
            share_copy(-2 * sign, h, core).start()
    for i, (sign, _) in enumerate(WAYS):
        own1_copy(i).wait_recv()
        share_copy(-sign, None, core).start()

    def back(first):
        def step(j, carry):
            at = pl.multiple_of(first * 192 + j * 128, 128)
            o_weights[:, pl.ds(at, 128)] = wt[pl.ds(at, 128), :].astype(F32).T.astype(BF16)
            return carry

        lax.fori_loop(0, 3, step, 0)

    share_copy(0, None, 1 - core).wait_recv()
    for sign, _ in WAYS:
        share_copy(-sign, None, 1 - core).wait_recv()
        for h in range(2):
            share_copy(-2 * sign, h, 1 - core).wait_recv()
    pair = y // 2
    back(2 * pair)
    back(2 * ((pair + turn + 4) % 4))
    for i, (sign, half) in enumerate(WAYS):
        fwd2_copy(i).wait_recv()
        share_copy(-4 * sign, half, core).start()
    for k in range(2):
        for i, (sign, half) in enumerate(WAYS):
            h = half if k == 0 else 1 - half
            fwd1_copy(i, h).wait_recv()
            share_copy(-3 * sign, h, core).start()
    for h in range(2):
        share_copy(-3 * turn, h, 1 - core).wait_recv()
    back(2 * ((pair - turn + 4) % 4))
    for off in (4, 3 * turn):
        for h in range(2):
            share_copy(off, h, 1 - core).wait_recv()
    back(2 * ((pair + 2) % 4))
    near = o_weights[pl.ds(pl.multiple_of(y * 2 * EROW, 16), 2 * EROW), :].astype(F32)
    row_block = jnp.where(core == 0, near[0:EROW], near[EROW:])
    o_ema[...] = 0.9 * e_v[...] + 0.1 * row_block

    for i, (sign, half) in enumerate(WAYS):
        own1_copy(i).wait_send()
        fwd2_copy(i).wait_send()
        share_copy(-sign, None, core).wait_send()
        share_copy(-4 * sign, half, core).wait_send()
        for h in range(2):
            fwd1_copy(i, h).wait_send()
            share_copy(-2 * sign, h, core).wait_send()
            share_copy(-3 * sign, h, core).wait_send()
    share_copy(0, None, core).wait_send()


def hand_over(*refs):
    sems = refs[-1]
    copies = [
        pltpu.make_async_copy(refs[i], refs[8 + i], sems.at[i]) for i in (4, 0, 1, 2, 3, 5, 6, 7)
    ]
    for copy in copies:
        copy.start()
    for copy in copies:
        copy.wait()


def body(grad_proj, grad_conv, param_proj, m_proj, v_proj, ema_proj, param_conv, m_conv, v_conv):
    small = jax.ShapeDtypeStruct((KCONV, CCOL), F32)
    block = jax.ShapeDtypeStruct((BLK, ROWS), F32)
    dma = pltpu.SemaphoreType.DMA
    outs = pl.pallas_call(
        kernel,
        out_shape=(
            block, block, block,
            jax.ShapeDtypeStruct((EROW, D), F32),
            jax.ShapeDtypeStruct((ROWS, D), BF16),
            small, small, small,
        ),
        in_specs=[pl.BlockSpec(memory_space=pltpu.HBM)] * 9,
        out_specs=[pl.BlockSpec(memory_space=pltpu.VMEM)] * 8,
        scratch_shapes=[
            pltpu.VMEM((ROWS, D), F32),
            pltpu.VMEM((D, ROWS), F32),
            pltpu.VMEM((YS, BLK, ROWS), BF16),
            pltpu.VMEM((YS, BLK, ROWS), BF16),
            pltpu.VMEM((2, HALF, ROWS), BF16),
            pltpu.VMEM((2, HALF, ROWS), BF16),
            pltpu.VMEM((4, HALF, ROWS), BF16),
            pltpu.VMEM((4, HALF, ROWS), BF16),
            pltpu.VMEM((4, HALF, ROWS), BF16),
            pltpu.VMEM((4, HALF, ROWS), BF16),
            pltpu.VMEM((4, HALF, ROWS), BF16),
            pltpu.VMEM((4, HALF, ROWS), BF16),
            pltpu.VMEM((2 * REPS, HALF, ROWS), BF16),
            pltpu.VMEM((D, ROWS), BF16),
            pltpu.VMEM((BLK, ROWS), F32),
            pltpu.VMEM((BLK, ROWS), F32),
            pltpu.VMEM((BLK, ROWS), F32),
            pltpu.VMEM((EROW, D), F32),
            pltpu.VMEM((YS, KCONV, CCOL), F32),
            pltpu.VMEM((2, KCONV, CCOL), F32),
            pltpu.VMEM((REPS, KCONV, CCOL), F32),
            pltpu.VMEM((KCONV, CCOL), F32),
            pltpu.VMEM((KCONV, CCOL), F32),
            pltpu.VMEM((KCONV, CCOL), F32),
            pltpu.VMEM((2 * YS, 8, 128), F32),
            pltpu.VMEM((TENS, 8, 128), F32),
            dma((12,)),
            dma((YS,)), dma((YS,)),
            dma((2,)), dma((2,)),
            dma((4,)), dma((4,)),
            dma((4,)), dma((4,)),
            dma((4,)), dma((4,)),
            dma((2 * REPS,)), dma((2 * REPS,)),
            dma((6,)), dma((6,)),
            dma((6,)), dma((6,)),
            dma((2 * YS,)), dma((2 * YS,)),
            dma((YS,)), dma((YS,)),
            dma, dma,
            dma((REPS,)), dma((REPS,)),
            dma((2 * YS,)), dma((2 * YS,)),
            dma((TENS,)), dma((TENS,)),
            pltpu.SemaphoreType.REGULAR, pltpu.SemaphoreType.REGULAR((2,)),
        ],
        compiler_params=pltpu.CompilerParams(
            collective_id=0, has_side_effects=True, vmem_limit_bytes=48 << 20
        ),
        name="adamw_step",
    )(
        *(
            pltpu.with_memory_space_constraint(x, pltpu.HBM)
            for x in (
                grad_proj[0], grad_conv[0], param_proj.T, m_proj.T, v_proj.T, ema_proj,
                param_conv, m_conv, v_conv,
            )
        )
    )
    outs = pl.pallas_call(
        hand_over,
        out_shape=tuple(jax.ShapeDtypeStruct(x.shape, x.dtype) for x in outs),
        in_specs=[pl.BlockSpec(memory_space=pltpu.VMEM)] * 8,
        out_specs=[pl.BlockSpec(memory_space=pltpu.HBM)] * 8,
        scratch_shapes=[dma((8,))],
        name="hand_over",
    )(*(pltpu.with_memory_space_constraint(x, pltpu.VMEM) for x in outs))
    new_param, new_m, new_v, new_ema, weights, new_cparam, new_cm, new_cv = outs
    return (new_param.T, new_m.T, new_v.T, new_ema, weights, new_cparam, new_cm, new_cv)


def solution(mesh):
    in_specs = (
        P(("rep", "dp"), "tensor", None),
        P(("rep", "dp"), None, "tensor"),
        P("tensor", "dp"),
        P("tensor", "dp"),
        P("tensor", "dp"),
        P(("tensor", "dp"), None),
        P(None, "tensor"),
        P(None, "tensor"),
        P(None, "tensor"),
    )
    out_specs = (
        P("tensor", "dp"),
        P("tensor", "dp"),
        P("tensor", "dp"),
        P(("tensor", "dp"), None),
        P("tensor", None),
        P(None, "tensor"),
        P(None, "tensor"),
        P(None, "tensor"),
    )
    return jax.shard_map(body, mesh=mesh, in_specs=in_specs, out_specs=out_specs, check_vma=False)
```

```python
import functools
import math

import jax
import jax.numpy as jnp
from jax import lax
from jax.experimental import pallas as pl
from jax.experimental.pallas import tpu as pltpu
from jax.sharding import PartitionSpec as P

D = 1536
INNER = 3072
CONV = 3328
KCONV = 4

F32 = jnp.float32
BF16 = jnp.bfloat16
MESH = pl.DeviceIdType.MESH

YS = 8
REPS = 4
TENS = 8
ROWS = INNER // TENS
BLK = D // (2 * YS)
HALF = BLK // 2
CCOL = CONV // TENS
EROW = ROWS // (2 * YS)
SCALE_UP = 2.0**15
SCALE_DOWN = 2.0**-15


def adamw_step(param_in, first_in, second_in, grad_in):
    first_out = 0.9 * first_in + 0.1 * grad_in
    second_out = 0.95 * second_in + 0.05 * grad_in * grad_in
    bias_one = 1.0 - 0.9**10
    bias_two = 1.0 - 0.95**10
    update = first_out / bias_one / (jnp.sqrt(second_out / bias_two) + 1e-08)
    param_out = param_in - 0.25 * (update + 0.1 * param_in)
    return (param_out, first_out, second_out)


def clip_from(square_sum):
    clip_limit = 0.5 * math.sqrt(INNER * D + KCONV * CONV)
    return jnp.minimum(1.0, clip_limit / (jnp.sqrt(square_sum) + 1e-06))


def encode(x):
    wide = x * SCALE_UP
    square = wide * wide
    return ((square * wide) * jnp.abs(wide)).astype(BF16)


def signed_root(x):
    return x * lax.rsqrt(jnp.maximum(jnp.abs(x), 1e-37))


def decode(code):
    return signed_root(signed_root(code.astype(F32))) * SCALE_DOWN


def fold(x):
    total = x[0:8, 0:128]
    for i in range(x.shape[0] // 8):
        for j in range(x.shape[1] // 128):
            if i or j:
                total = total + x[8 * i : 8 * i + 8, 128 * j : 128 * j + 128]
    return total


WAYS = ((1, 0), (-1, 1))


def kernel(
    grad, conv, param, mom, vel, ema, cparam, cmom, cvel,
    o_param, o_mom, o_vel, o_ema, o_weights, o_cparam, o_cmom, o_cvel,
    g_in, gt, pair_out, pair_in, far_out, far_in, mid_out, mid_in, rel_out, rel_in, near_out, near_in,
    zx, wt, p_v, m_v, v_v, e_v, conv_y, conv_c, conv_z, cp_v, cm_v, cv_v, norm_d, norm_t,
    load_sem, pair_s, pair_r, step_s, mid_s, far_r, mid_r, rel_r, near_r, zx_s, zx_r,
    own_s, own_r, fwd_s, fwd_r, share_s, share_r, cy_s, cy_r, cc_s, cc_r, cz_s, cz_r,
    nd_s, nd_r, nt_s, nt_r, hello_z, hello_x,
):
    rep = lax.axis_index("rep")
    dp = lax.axis_index("dp")
    ten = lax.axis_index("tensor")
    y = dp // 2
    core = dp % 2
    partner = 2 * y + (1 - core)

    def y_at(off):
        return (y + off + YS) % YS

    def remote(src, dst, send, recv, **device):
        return pltpu.make_async_remote_copy(
            src_ref=src, dst_ref=dst, send_sem=send, recv_sem=recv,
            device_id=device, device_id_type=MESH,
        )

    def sent(ref, sem):
        remote(ref, ref, sem, cc_r, dp=partner).wait_send()

    def landed(ref, sem):
        remote(ref, ref, cc_s, sem, dp=partner).wait_recv()

    def wt_rows(n):
        return wt.at[pl.ds(0, n), :]

    base = (y // 2 + 2) % 4
    turn = 2 * (y % 2) - 1
    order = (base, (base + turn + 4) % 4, (base - turn + 4) % 4, (base + 2) % 4)
    loads = []
    for i, group in enumerate(order):
        cols = pl.ds(pl.multiple_of(group * 384, 128), 384)
        loads.append(pltpu.make_async_copy(grad.at[:, cols], g_in.at[:, cols], load_sem.at[i]))
    for copy in loads:
        copy.start()
    conv_load = pltpu.make_async_copy(conv, conv_z.at[rep], load_sem.at[4])
    late = []
    for i, (src, dst) in enumerate(
        ((param, p_v), (mom, m_v), (vel, v_v), (ema, e_v), (cparam, cp_v), (cmom, cm_v), (cvel, cv_v))
    ):
        late.append(pltpu.make_async_copy(src, dst, load_sem.at[5 + i]))

    x_near = [{"tensor": (ten + 2) % TENS}, {"tensor": (ten + TENS - 2) % TENS}, {"tensor": ten + 1 - 2 * (ten % 2)}]
    z_near = [{"rep": (rep + 1) % REPS}, {"rep": (rep + REPS - 1) % REPS}]
    y_near = [{"dp": 2 * y_at(off) + core} for off in (2, -2, 1, -1)]
    barrier = pltpu.get_barrier_semaphore()

    def signal(sem, devices):
        for device in devices:
            pl.semaphore_signal(sem, inc=1, device_id=device, device_id_type=MESH)

    signal(barrier, y_near[:2] + z_near + y_near[2:] + x_near + [{"dp": partner}])

    def turn_group(i):
        loads[i].wait()
        group = order[i]

        def step(j, carry):
            at = pl.multiple_of(group * 384 + j * 128, 128)
            gt[pl.ds(at, 128), :] = g_in[:, pl.ds(at, 128)].T
            return carry

        lax.fori_loop(0, 3, step, 0)
        for k in range(2):
            own = 2 * group + k
            rows = pl.ds(pl.multiple_of((2 * own + (1 - core)) * BLK, BLK), BLK)
            pair_out[own] = encode(gt[rows, :])

    def pair_copy(own):
        return remote(
            pair_out.at[own], pair_in.at[own], pair_s, pair_r.at[own], dp=partner
        )

    def conv_y_copy(off):
        return remote(
            conv_y.at[y], conv_y.at[y], cy_s, cy_r, dp=2 * y_at(off) + core
        )

    for copy in [conv_load] + late:
        copy.start()
    for i in range(4):
        turn_group(i)
    pl.semaphore_wait(barrier, 10)
    def pair_start(groups):
        for i in groups:
            for k in range(2):
                pair_copy(2 * order[i] + k).start()

    pair_start((0, 1))
    signal(hello_z, z_near)
    signal(hello_x.at[0], x_near)

    arrived = set()

    def local_sum(off, half=None):
        own = y_at(off)
        if off % YS not in arrived:
            arrived.add(off % YS)
            pair_copy(own).wait_recv()
        lo, n = (0, BLK) if half is None else (half * HALF, HALF)
        rows = pl.ds(pl.multiple_of((2 * own + core) * BLK + lo, 16), n)
        return gt[rows, :] + decode(pair_in[own, lo : lo + n, :])

    def y_copy(out, into, i, send, recv, hops):
        return remote(out.at[i], into.at[i], send, recv, dp=2 * y_at(hops) + core)

    def far_copy(i):
        return y_copy(far_out, far_in, i, step_s, far_r.at[i], 2 * WAYS[i][0])

    def mid_copy(i, half):
        send = mid_s if half else step_s
        return y_copy(mid_out, mid_in, 2 * i + half, send, mid_r.at[2 * i + half], WAYS[i][0])

    def rel_copy(i, half):
        return y_copy(rel_out, rel_in, 2 * i + half, step_s, rel_r.at[half], 2 * WAYS[i][0])

    def near_copy(i, half):
        return y_copy(near_out, near_in, 2 * i + half, step_s, near_r.at[half], WAYS[i][0])

    def conv_c_copy():
        return remote(conv_c.at[core], conv_c.at[core], cc_s, cc_r, dp=partner)

    def conv_z_copy(off):
        return remote(
            conv_z.at[rep], conv_z.at[rep], cz_s, cz_r, rep=(rep + off) % REPS
        )

    for i, (sign, half) in enumerate(WAYS):
        far_out[i] = encode(local_sum(4 * sign, half))
        far_copy(i).start()
    for h in range(2):
        for i, (sign, _) in enumerate(WAYS):
            mid_out[2 * i + h] = encode(local_sum(3 * sign, h))
            mid_copy(i, h).start()
    pair_start((2, 3))
    for h in range(2):
        for i, (sign, _) in enumerate(WAYS):
            near_out[2 * i + h] = encode(local_sum(sign, h))
    sent(wt_rows(2 * HALF), mid_s)
    for h in range(2):
        for i in range(2):
            near_copy(i, h).start()
    for i, h in ((0, 0), (1, 0), (1, 1), (0, 1)):
        mid_copy(i, h).wait_recv()
        total = local_sum(2 * WAYS[i][0], h) + decode(mid_in[2 * i + h])
        if h == WAYS[i][1]:
            far_copy(i).wait_recv()
            total = total + decode(far_in[i])
        rel_out[2 * i + h] = encode(total)
        rel_copy(i, h).start()
    conv_load.wait()
    pl.semaphore_wait(hello_z, 2)
    for off in range(1, REPS):
        conv_z_copy(off).start()
    pl.semaphore_wait(hello_x.at[0], 3)
    signal(hello_x.at[1], x_near)

    def zx_copy(off, h):
        return remote(
            zx.at[2 * rep + h], zx.at[2 * rep + h], zx_s, zx_r.at[h],
            rep=(rep + off) % REPS,
        )

    for h in range(2):
        total = local_sum(0, h)
        landed(near_in.at[pl.ds(0, 2)], near_r.at[h])
        for i in range(2):
            total = total + decode(near_in[2 * i + h])
        landed(rel_in.at[pl.ds(0, 2)], rel_r.at[h])
        for i in range(2):
            total = total + decode(rel_in[2 * i + h])
        zx[2 * rep + h] = encode(total)
        for off in (2, 1, 3):
            zx_copy(off, h).start()

    count = float(REPS * 2 * YS)
    landed(conv_z.at[pl.ds(0, REPS - 1)], cz_r)
    conv_y[y] = ((conv_z[0] + conv_z[1]) + conv_z[2]) + conv_z[3]
    for off in range(1, YS):
        conv_y_copy(off).start()

    avg = []
    for h in range(2):
        landed(zx.at[pl.ds(0, REPS - 1)], zx_r.at[h])
        total = decode(zx[h])
        for r in range(1, REPS):
            total = total + decode(zx[2 * r + h])
        avg.append(total * (1.0 / count))
        if h == 0:
            landed(conv_y.at[pl.ds(0, YS - 1)], cy_r)
            total = conv_y[0]
            for i in range(1, YS):
                total = total + conv_y[i]
            conv_c[core] = total
            conv_c_copy().start()

    def rows_at(buf, first, n):
        return buf.at[pl.ds(first, n), pl.ds(0, 1), :]

    def spread(buf, send, recv, axis, me, size):
        def start(i, carry):
            at = rows_at(buf, me, 1)
            remote(at, at, send, recv, **{axis: (me + i) % size}).start()
            return carry

        lax.fori_loop(1, size, start, 0)

    def collect(buf, recv, size):
        landed(rows_at(buf, 0, size - 1), recv)
        total = buf[0, 0:1, :]
        for i in range(1, size):
            total = total + buf[i, 0:1, :]
        return total

    square = fold(avg[0] * avg[0]) + fold(avg[1] * avg[1])
    norm_d[dp, 0:1, :] = jnp.sum(square, axis=0, keepdims=True)
    spread(norm_d, nd_s, nd_r, "dp", dp, 2 * YS)
    for h in range(2):
        gt[h * HALF : (h + 1) * HALF, :] = avg[h]
    for copy in late:
        copy.wait()
    conv_c_copy().wait_recv()
    conv_avg = (conv_c[0] + conv_c[1]) * (1.0 / count)
    conv_square = jnp.sum(conv_avg * conv_avg)
    pl.semaphore_wait(hello_x.at[1], 3)
    norm_t[ten, 0:1, :] = collect(norm_d, nd_r, 2 * YS) + conv_square * (1.0 / 128.0)
    spread(norm_t, nt_s, nt_r, "tensor", ten, TENS)

    square_sum = jnp.sum(collect(norm_t, nt_r, TENS), keepdims=True)
    clip = clip_from(square_sum)

    new_param, new_mom, new_vel = adamw_step(p_v[...], m_v[...], v_v[...], clip * gt[0:BLK, :])
    mine = pl.multiple_of(dp * BLK, BLK)
    wt[pl.ds(mine, BLK), :] = new_param.astype(BF16)

    def rows_of(off, whose, half=None):
        lo, n = (0, BLK) if half is None else (half * HALF, HALF)
        return pl.ds(pl.multiple_of((2 * y_at(off) + whose) * BLK + lo, 16), n)

    def gather_copy(send, recv, slot, off, half, hops):
        rows = rows_of(off, core, half)
        return remote(
            wt.at[rows, :], wt.at[rows, :], send, recv.at[slot], dp=2 * y_at(hops) + core
        )

    def own2_copy(i, half):
        return gather_copy(own_s, own_r, 2 * i + half, 0, half, 2 * WAYS[i][0])

    def own1_copy(i):
        return gather_copy(fwd_s, own_r, 4 + i, 0, None, WAYS[i][0])

    def fwd1_copy(i, half):
        return gather_copy(fwd_s, fwd_r, 2 * i + half, -2 * WAYS[i][0], half, WAYS[i][0])

    def fwd2_copy(i):
        sign, half = WAYS[i]
        return gather_copy(fwd_s, fwd_r, 4 + i, -2 * sign, half, 2 * sign)

    def share_copy(off, half):
        rows = rows_of(off, core, half)
        slot = 0 if abs(off) <= 2 else 2 if off == 4 else (3 - turn * (-off // 3)) // 2
        return remote(wt.at[rows, :], wt.at[rows, :], share_s, share_r.at[slot], dp=partner)

    for k in range(2):
        for i, (sign, half) in enumerate(WAYS):
            own2_copy(i, half if k == 0 else 1 - half).start()
    share_copy(0, None).start()

    o_param[...] = new_param
    o_mom[...] = new_mom
    o_vel[...] = new_vel
    new_cparam, new_cmom, new_cvel = adamw_step(cp_v[...], cm_v[...], cv_v[...], clip * conv_avg)
    o_cparam[...] = new_cparam
    o_cmom[...] = new_cmom
    o_cvel[...] = new_cvel

    sent(wt_rows(4 * HALF), own_s)
    for i in range(2):
        own1_copy(i).start()

    sent(pair_out, pair_s)
    sent(wt_rows(12 * HALF), step_s)
    sent(conv_y.at[pl.ds(0, YS - 1)], cy_s)
    conv_c_copy().wait_send()
    sent(conv_z.at[pl.ds(0, REPS - 1)], cz_s)
    sent(zx.at[pl.ds(0, 2 * (REPS - 1))], zx_s)
    sent(rows_at(norm_d, 0, 2 * YS - 1), nd_s)
    sent(rows_at(norm_t, 0, TENS - 1), nt_s)

    for k in range(2):
        for i, (sign, half) in enumerate(WAYS):
            h = half if k == 0 else 1 - half
            own2_copy(i, h).wait_recv()
            if k == 0:
                fwd2_copy(i).start()
            fwd1_copy(i, h).start()
            share_copy(-2 * sign, h).start()
    for i, (sign, _) in enumerate(WAYS):
        own1_copy(i).wait_recv()
        share_copy(-sign, None).start()

    def back(first):
        def step(j, carry):
            at = pl.multiple_of(first * 192 + j * 128, 128)
            o_weights[:, pl.ds(at, 128)] = wt[pl.ds(at, 128), :].T
            return carry

        lax.fori_loop(0, 3, step, 0)

    for i, (sign, half) in enumerate(WAYS):
        fwd2_copy(i).wait_recv()
        share_copy(4, half).start()
    for k in range(2):
        for i, (sign, half) in enumerate(WAYS):
            h = half if k == 0 else 1 - half
            fwd1_copy(i, h).wait_recv()
            share_copy(-3 * sign, h).start()
    landed(wt_rows(5 * BLK), share_r.at[0])
    pair = y // 2
    back(2 * pair)
    back(2 * ((pair + turn + 4) % 4))
    landed(wt_rows(BLK), share_r.at[1])
    back(2 * ((pair - turn + 4) % 4))
    landed(wt_rows(2 * BLK), share_r.at[2])
    back(2 * ((pair + 2) % 4))
    near = o_weights[pl.ds(pl.multiple_of(y * 2 * EROW, 16), 2 * EROW), :].astype(F32)
    row_block = jnp.where(core == 0, near[0:EROW], near[EROW:])
    o_ema[...] = 0.9 * e_v[...] + 0.1 * row_block

    sent(wt_rows(10 * HALF), fwd_s)
    sent(wt_rows(8 * BLK), share_s)


def hand_over(*refs):
    sems = refs[-1]
    copies = [
        pltpu.make_async_copy(refs[i], refs[8 + i], sems.at[i]) for i in (4, 0, 1, 2, 3, 5, 6, 7)
    ]
    for copy in copies:
        copy.start()
    for copy in copies:
        copy.wait()


def body(grad_proj, grad_conv, param_proj, m_proj, v_proj, ema_proj, param_conv, m_conv, v_conv):
    small = jax.ShapeDtypeStruct((KCONV, CCOL), F32)
    block = jax.ShapeDtypeStruct((BLK, ROWS), F32)
    dma = pltpu.SemaphoreType.DMA
    outs = pl.pallas_call(
        kernel,
        out_shape=(
            block, block, block,
            jax.ShapeDtypeStruct((EROW, D), F32),
            jax.ShapeDtypeStruct((ROWS, D), BF16),
            small, small, small,
        ),
        in_specs=[pl.BlockSpec(memory_space=pltpu.HBM)] * 9,
        out_specs=[pl.BlockSpec(memory_space=pltpu.VMEM)] * 8,
        scratch_shapes=[
            pltpu.VMEM((ROWS, D), F32),
            pltpu.VMEM((D, ROWS), F32),
            pltpu.VMEM((YS, BLK, ROWS), BF16),
            pltpu.VMEM((YS, BLK, ROWS), BF16),
            pltpu.VMEM((2, HALF, ROWS), BF16),
            pltpu.VMEM((2, HALF, ROWS), BF16),
            pltpu.VMEM((4, HALF, ROWS), BF16),
            pltpu.VMEM((4, HALF, ROWS), BF16),
            pltpu.VMEM((4, HALF, ROWS), BF16),
            pltpu.VMEM((4, HALF, ROWS), BF16),
            pltpu.VMEM((4, HALF, ROWS), BF16),
            pltpu.VMEM((4, HALF, ROWS), BF16),
            pltpu.VMEM((2 * REPS, HALF, ROWS), BF16),
            pltpu.VMEM((D, ROWS), BF16),
            pltpu.VMEM((BLK, ROWS), F32),
            pltpu.VMEM((BLK, ROWS), F32),
            pltpu.VMEM((BLK, ROWS), F32),
            pltpu.VMEM((EROW, D), F32),
            pltpu.VMEM((YS, KCONV, CCOL), F32),
            pltpu.VMEM((2, KCONV, CCOL), F32),
            pltpu.VMEM((REPS, KCONV, CCOL), F32),
            pltpu.VMEM((KCONV, CCOL), F32),
            pltpu.VMEM((KCONV, CCOL), F32),
            pltpu.VMEM((KCONV, CCOL), F32),
            pltpu.VMEM((2 * YS, 8, 128), F32),
            pltpu.VMEM((TENS, 8, 128), F32),
            dma((12,)),
            dma, dma((YS,)),
            dma, dma,
            dma((2,)), dma((4,)), dma((2,)), dma((2,)),
            dma, dma((2,)),
            dma, dma((6,)),
            dma, dma((6,)),
            dma, dma((3,)),
            dma, dma,
            dma, dma,
            dma, dma,
            dma, dma,
            dma, dma,
            pltpu.SemaphoreType.REGULAR, pltpu.SemaphoreType.REGULAR((2,)),
        ],
        compiler_params=pltpu.CompilerParams(
            collective_id=0, has_side_effects=True, vmem_limit_bytes=48 << 20
        ),
        name="adamw_step",
    )(
        *(
            pltpu.with_memory_space_constraint(x, pltpu.HBM)
            for x in (
                grad_proj[0], grad_conv[0], param_proj.T, m_proj.T, v_proj.T, ema_proj,
                param_conv, m_conv, v_conv,
            )
        )
    )
    outs = pl.pallas_call(
        hand_over,
        out_shape=tuple(jax.ShapeDtypeStruct(x.shape, x.dtype) for x in outs),
        in_specs=[pl.BlockSpec(memory_space=pltpu.VMEM)] * 8,
        out_specs=[pl.BlockSpec(memory_space=pltpu.HBM)] * 8,
        scratch_shapes=[dma((8,))],
        name="hand_over",
    )(*(pltpu.with_memory_space_constraint(x, pltpu.VMEM) for x in outs))
    new_param, new_m, new_v, new_ema, weights, new_cparam, new_cm, new_cv = outs
    return (new_param.T, new_m.T, new_v.T, new_ema, weights, new_cparam, new_cm, new_cv)


def solution(mesh):
    in_specs = (
        P(("rep", "dp"), "tensor", None),
        P(("rep", "dp"), None, "tensor"),
        P("tensor", "dp"),
        P("tensor", "dp"),
        P("tensor", "dp"),
        P(("tensor", "dp"), None),
        P(None, "tensor"),
        P(None, "tensor"),
        P(None, "tensor"),
    )
    out_specs = (
        P("tensor", "dp"),
        P("tensor", "dp"),
        P("tensor", "dp"),
        P(("tensor", "dp"), None),
        P("tensor", None),
        P(None, "tensor"),
        P(None, "tensor"),
        P(None, "tensor"),
    )
    return jax.shard_map(body, mesh=mesh, in_specs=in_specs, out_specs=out_specs, check_vma=False)
```

```python
import functools
import math

import jax
import jax.numpy as jnp
from jax import lax
from jax.experimental import pallas as pl
from jax.experimental.pallas import tpu as pltpu
from jax.sharding import PartitionSpec as P

D = 1536
INNER = 3072
CONV = 3328
KCONV = 4

F32 = jnp.float32
BF16 = jnp.bfloat16
MESH = pl.DeviceIdType.MESH

YS = 8
REPS = 4
TENS = 8
ROWS = INNER // TENS
BLK = D // (2 * YS)
HALF = BLK // 2
CCOL = CONV // TENS
EROW = ROWS // (2 * YS)
SCALE_UP = 2.0**15
SCALE_DOWN = 2.0**-15


def adamw_step(param_in, first_in, second_in, grad_in):
    first_out = 0.9 * first_in + 0.1 * grad_in
    second_out = 0.95 * second_in + 0.05 * grad_in * grad_in
    bias_one = 1.0 - 0.9**10
    bias_two = 1.0 - 0.95**10
    update = first_out / bias_one / (jnp.sqrt(second_out / bias_two) + 1e-08)
    param_out = param_in - 0.25 * (update + 0.1 * param_in)
    return (param_out, first_out, second_out)


def clip_from(square_sum):
    clip_limit = 0.5 * math.sqrt(INNER * D + KCONV * CONV)
    return jnp.minimum(1.0, clip_limit / (jnp.sqrt(square_sum) + 1e-06))


def encode(x):
    wide = x * SCALE_UP
    square = wide * wide
    return ((square * wide) * jnp.abs(wide)).astype(BF16)


def signed_root(x):
    return x * lax.rsqrt(jnp.maximum(jnp.abs(x), 1e-37))


def decode(code):
    return signed_root(signed_root(code.astype(F32))) * SCALE_DOWN


def fold(x):
    total = x[0:8, 0:128]
    for i in range(x.shape[0] // 8):
        for j in range(x.shape[1] // 128):
            if i or j:
                total = total + x[8 * i : 8 * i + 8, 128 * j : 128 * j + 128]
    return total


WAYS = ((1, 0), (-1, 1))


def kernel(
    grad, conv, param, mom, vel, ema, cparam, cmom, cvel,
    o_param, o_mom, o_vel, o_ema, o_weights, o_cparam, o_cmom, o_cvel,
    g_in, gt, pair_out, pair_in, far_out, far_in, mid_out, mid_in, rel_out, rel_in, near_out, near_in,
    zx, wt, state, e_v, conv_y, conv_c, conv_z, cstate, norm_d, norm_t,
    load_sem, pair_s, pair_r, step_s, mid_s, mid_r, rel_r, near_r, zx_s, zx_r,
    own_s, own_r, fwd_s, fwd_r, share_s, share_r, cy_s, cy_r, cc_s, cc_r, cz_s, cz_r,
    nd_s, nd_r, nt_s, nt_r, hello_z, hello_x,
):
    rep = lax.axis_index("rep")
    dp = lax.axis_index("dp")
    ten = lax.axis_index("tensor")
    y = dp // 2
    core = dp % 2
    partner = 2 * y + (1 - core)

    def y_at(off):
        return (y + off + YS) % YS

    def remote(src, dst, send, recv, **device):
        return pltpu.make_async_remote_copy(
            src_ref=src, dst_ref=dst, send_sem=send, recv_sem=recv,
            device_id=device, device_id_type=MESH,
        )

    def sent(ref, sem):
        remote(ref, ref, sem, cc_r, dp=partner).wait_send()

    def landed(ref, sem):
        remote(ref, ref, cc_s, sem, dp=partner).wait_recv()

    def wt_rows(n):
        return wt.at[pl.ds(0, n), :]

    base = (y // 2 + 2) % 4
    turn = 2 * (y % 2) - 1
    order = (base, (base + turn + 4) % 4, (base - turn + 4) % 4, (base + 2) % 4)
    loads = []
    for i, group in enumerate(order):
        cols = pl.ds(pl.multiple_of(group * 384, 128), 384)
        loads.append(pltpu.make_async_copy(grad.at[:, cols], g_in.at[:, cols], load_sem.at[i]))
    for copy in loads:
        copy.start()
    conv_load = pltpu.make_async_copy(conv, conv_z.at[rep], load_sem.at[4])
    late = []
    for src, dst, i in (
        (param, state.at[0], 5), (mom, state.at[1], 5), (vel, state.at[2], 5), (ema, e_v, 6),
        (cparam, cstate.at[0], 7), (cmom, cstate.at[1], 7), (cvel, cstate.at[2], 7),
    ):
        late.append(pltpu.make_async_copy(src, dst, load_sem.at[i]))

    x_near = [{"tensor": (ten + 2) % TENS}, {"tensor": (ten + TENS - 2) % TENS}, {"tensor": ten + 1 - 2 * (ten % 2)}]
    z_near = [{"rep": (rep + 1) % REPS}, {"rep": (rep + REPS - 1) % REPS}]
    y_near = [{"dp": 2 * y_at(off) + core} for off in (2, -2, 1, -1)]
    barrier = pltpu.get_barrier_semaphore()

    def signal(sem, devices):
        for device in devices:
            pl.semaphore_signal(sem, inc=1, device_id=device, device_id_type=MESH)

    signal(barrier, y_near[:2] + z_near + y_near[2:] + x_near + [{"dp": partner}])

    def turn_group(i):
        loads[i].wait()
        group = order[i]

        def step(j, carry):
            at = pl.multiple_of(group * 384 + j * 128, 128)
            gt[pl.ds(at, 128), :] = g_in[:, pl.ds(at, 128)].T
            return carry

        lax.fori_loop(0, 3, step, 0)
        for k in range(2):
            own = 2 * group + k
            rows = pl.ds(pl.multiple_of((2 * own + (1 - core)) * BLK, BLK), BLK)
            pair_out[own] = encode(gt[rows, :])

    def pair_copy(own):
        return remote(
            pair_out.at[own], pair_in.at[own], pair_s, pair_r.at[own], dp=partner
        )

    def conv_y_copy(off):
        return remote(
            conv_y.at[y], conv_y.at[y], cy_s, cy_r, dp=2 * y_at(off) + core
        )

    for copy in [conv_load] + late:
        copy.start()
    for i in range(4):
        turn_group(i)
    pl.semaphore_wait(barrier, 10)
    def pair_start(groups):
        for i in groups:
            for k in range(2):
                pair_copy(2 * order[i] + k).start()

    pair_start((0, 1))
    signal(hello_z, z_near)
    signal(hello_x.at[0], x_near)

    arrived = set()

    def local_sum(off, half=None):
        own = y_at(off)
        if off % YS not in arrived:
            arrived.add(off % YS)
            pair_copy(own).wait_recv()
        lo, n = (0, BLK) if half is None else (half * HALF, HALF)
        rows = pl.ds(pl.multiple_of((2 * own + core) * BLK + lo, 16), n)
        return gt[rows, :] + decode(pair_in[own, lo : lo + n, :])

    def y_copy(out, into, i, send, recv, hops):
        return remote(out.at[i], into.at[i], send, recv, dp=2 * y_at(hops) + core)

    def far_copy(i):
        return y_copy(far_out, far_in, i, step_s, mid_r.at[i], 2 * WAYS[i][0])

    def mid_copy(i, half):
        send = mid_s if half else step_s
        return y_copy(mid_out, mid_in, 2 * i + half, send, mid_r.at[half], WAYS[i][0])

    def rel_copy(i, half):
        return y_copy(rel_out, rel_in, 2 * i + half, step_s, rel_r.at[half], 2 * WAYS[i][0])

    def near_copy(i, half):
        return y_copy(near_out, near_in, 2 * i + half, step_s, near_r.at[half], WAYS[i][0])

    def conv_c_copy():
        return remote(conv_c.at[core], conv_c.at[core], cc_s, cc_r, dp=partner)

    def conv_z_copy(off):
        return remote(
            conv_z.at[rep], conv_z.at[rep], cz_s, cz_r, rep=(rep + off) % REPS
        )

    for i, (sign, half) in enumerate(WAYS):
        far_out[i] = encode(local_sum(4 * sign, half))
        far_copy(i).start()
    for h in range(2):
        for i, (sign, _) in enumerate(WAYS):
            mid_out[2 * i + h] = encode(local_sum(3 * sign, h))
            mid_copy(i, h).start()
    pair_start((2, 3))
    for h in range(2):
        for i, (sign, _) in enumerate(WAYS):
            near_out[2 * i + h] = encode(local_sum(sign, h))
    sent(wt_rows(2 * HALF), mid_s)
    for h in range(2):
        for i in range(2):
            near_copy(i, h).start()
    for i, h in ((0, 0), (1, 0), (1, 1), (0, 1)):
        if i == h:
            landed(wt_rows(3 * HALF), mid_r.at[h])
        total = local_sum(2 * WAYS[i][0], h) + decode(mid_in[2 * i + h])
        if h == WAYS[i][1]:
            total = total + decode(far_in[i])
        rel_out[2 * i + h] = encode(total)
        rel_copy(i, h).start()
    conv_load.wait()
    pl.semaphore_wait(hello_z, 2)
    for off in range(1, REPS):
        conv_z_copy(off).start()
    pl.semaphore_wait(hello_x.at[0], 3)
    signal(hello_x.at[1], x_near)

    def zx_copy(off, h):
        return remote(
            zx.at[2 * rep + h], zx.at[2 * rep + h], zx_s, zx_r.at[h],
            rep=(rep + off) % REPS,
        )

    for h in range(2):
        total = local_sum(0, h)
        landed(near_in.at[pl.ds(0, 2)], near_r.at[h])
        for i in range(2):
            total = total + decode(near_in[2 * i + h])
        landed(rel_in.at[pl.ds(0, 2)], rel_r.at[h])
        for i in range(2):
            total = total + decode(rel_in[2 * i + h])
        zx[2 * rep + h] = encode(total)
        for off in (2, 1, 3):
            zx_copy(off, h).start()

    count = float(REPS * 2 * YS)
    landed(conv_z.at[pl.ds(0, REPS - 1)], cz_r)
    conv_y[y] = ((conv_z[0] + conv_z[1]) + conv_z[2]) + conv_z[3]
    for off in range(1, YS):
        conv_y_copy(off).start()

    avg = []
    for h in range(2):
        landed(zx.at[pl.ds(0, REPS - 1)], zx_r.at[h])
        total = decode(zx[h])
        for r in range(1, REPS):
            total = total + decode(zx[2 * r + h])
        avg.append(total * (1.0 / count))
        if h == 0:
            landed(conv_y.at[pl.ds(0, YS - 1)], cy_r)
            total = conv_y[0]
            for i in range(1, YS):
                total = total + conv_y[i]
            conv_c[core] = total
            conv_c_copy().start()

    def rows_at(buf, first, n):
        return buf.at[pl.ds(first, n), pl.ds(0, 1), :]

    def spread(buf, send, recv, axis, me, size):
        at = rows_at(buf, me, 1)
        for i in sorted(range(1, size), key=lambda i: abs(i - size // 2)):
            remote(at, at, send, recv, **{axis: (me + i) % size}).start()

    def collect(buf, recv, size):
        landed(rows_at(buf, 0, size - 1), recv)
        total = buf[0, 0:1, :]
        for i in range(1, size):
            total = total + buf[i, 0:1, :]
        return total

    square = fold(avg[0] * avg[0]) + fold(avg[1] * avg[1])
    norm_d[dp, 0:1, :] = jnp.sum(square, axis=0, keepdims=True)
    spread(norm_d, nd_s, nd_r, "dp", dp, 2 * YS)
    for h in range(2):
        gt[h * HALF : (h + 1) * HALF, :] = avg[h]
    for ref, i in ((state, 5), (e_v, 6), (cstate, 7)):
        pltpu.make_async_copy(ref, ref, load_sem.at[i]).wait()
    conv_c_copy().wait_recv()
    conv_avg = (conv_c[0] + conv_c[1]) * (1.0 / count)
    conv_square = jnp.sum(conv_avg * conv_avg)
    pl.semaphore_wait(hello_x.at[1], 3)
    norm_t[ten, 0:1, :] = collect(norm_d, nd_r, 2 * YS) + conv_square * (1.0 / 128.0)
    spread(norm_t, nt_s, nt_r, "tensor", ten, TENS)

    square_sum = jnp.sum(collect(norm_t, nt_r, TENS), keepdims=True)
    clip = clip_from(square_sum)

    new_param, new_mom, new_vel = adamw_step(state[0], state[1], state[2], clip * gt[0:BLK, :])
    mine = pl.multiple_of(dp * BLK, BLK)
    wt[pl.ds(mine, BLK), :] = new_param.astype(BF16)

    def rows_of(off, whose, half=None):
        lo, n = (0, BLK) if half is None else (half * HALF, HALF)
        return pl.ds(pl.multiple_of((2 * y_at(off) + whose) * BLK + lo, 16), n)

    def gather_copy(send, recv, slot, off, half, hops):
        rows = rows_of(off, core, half)
        return remote(
            wt.at[rows, :], wt.at[rows, :], send, recv.at[slot], dp=2 * y_at(hops) + core
        )

    def own2_copy(i, half):
        return gather_copy(own_s, own_r, 2 * i + half, 0, half, 2 * WAYS[i][0])

    def own1_copy(i):
        return gather_copy(fwd_s, own_r, 4 + i, 0, None, WAYS[i][0])

    def fwd1_copy(i, half):
        return gather_copy(fwd_s, fwd_r, half if i == 0 else 1 - half, -2 * WAYS[i][0], half, WAYS[i][0])

    def fwd2_copy(i):
        sign, half = WAYS[i]
        return gather_copy(fwd_s, fwd_r, 2, -2 * sign, half, 2 * sign)

    def share_copy(off, half):
        rows = rows_of(off, core, half)
        slot = 0 if abs(off) <= 2 else 2 if off == 4 else (3 - turn * (-off // 3)) // 2
        return remote(wt.at[rows, :], wt.at[rows, :], share_s, share_r.at[slot], dp=partner)

    for k in range(2):
        for i, (sign, half) in enumerate(WAYS):
            own2_copy(i, half if k == 0 else 1 - half).start()
    share_copy(0, None).start()

    o_param[...] = new_param
    o_mom[...] = new_mom
    o_vel[...] = new_vel
    new_cparam, new_cmom, new_cvel = adamw_step(cstate[0], cstate[1], cstate[2], clip * conv_avg)
    o_cparam[...] = new_cparam
    o_cmom[...] = new_cmom
    o_cvel[...] = new_cvel

    sent(wt_rows(4 * HALF), own_s)
    for i in range(2):
        own1_copy(i).start()

    sent(pair_out, pair_s)
    sent(wt_rows(12 * HALF), step_s)
    sent(conv_y.at[pl.ds(0, YS - 1)], cy_s)
    conv_c_copy().wait_send()
    sent(conv_z.at[pl.ds(0, REPS - 1)], cz_s)
    sent(zx.at[pl.ds(0, 2 * (REPS - 1))], zx_s)
    sent(rows_at(norm_d, 0, 2 * YS - 1), nd_s)
    sent(rows_at(norm_t, 0, TENS - 1), nt_s)

    for k in range(2):
        for i, (sign, half) in enumerate(WAYS):
            h = half if k == 0 else 1 - half
            own2_copy(i, h).wait_recv()
            if k == 0:
                fwd2_copy(i).start()
            fwd1_copy(i, h).start()
            share_copy(-2 * sign, h).start()
    for i, (sign, _) in enumerate(WAYS):
        own1_copy(i).wait_recv()
        share_copy(-sign, None).start()

    def back(first):
        def step(j, carry):
            at = pl.multiple_of(first * 192 + j * 128, 128)
            o_weights[:, pl.ds(at, 128)] = wt[pl.ds(at, 128), :].T
            return carry

        lax.fori_loop(0, 3, step, 0)

    landed(wt_rows(2 * HALF), fwd_r.at[2])
    for i, (_, half) in enumerate(WAYS):
        share_copy(4, half).start()
    for k in range(2):
        landed(wt_rows(2 * HALF), fwd_r.at[k])
        for i, (sign, half) in enumerate(WAYS):
            share_copy(-3 * sign, half if k == 0 else 1 - half).start()
    landed(wt_rows(5 * BLK), share_r.at[0])
    pair = y // 2
    back(2 * pair)
    back(2 * ((pair + turn + 4) % 4))
    landed(wt_rows(BLK), share_r.at[1])
    back(2 * ((pair - turn + 4) % 4))
    landed(wt_rows(2 * BLK), share_r.at[2])
    back(2 * ((pair + 2) % 4))
    near = o_weights[pl.ds(pl.multiple_of(y * 2 * EROW, 16), 2 * EROW), :].astype(F32)
    row_block = jnp.where(core == 0, near[0:EROW], near[EROW:])
    o_ema[...] = 0.9 * e_v[...] + 0.1 * row_block

    sent(wt_rows(10 * HALF), fwd_s)
    sent(wt_rows(8 * BLK), share_s)


def hand_over(*refs):
    sems = refs[-1]
    copies = [
        pltpu.make_async_copy(refs[i], refs[8 + i], sems.at[i]) for i in (4, 0, 1, 2, 3, 5, 6, 7)
    ]
    for copy in copies:
        copy.start()
    for copy in copies:
        copy.wait()


def body(grad_proj, grad_conv, param_proj, m_proj, v_proj, ema_proj, param_conv, m_conv, v_conv):
    small = jax.ShapeDtypeStruct((KCONV, CCOL), F32)
    block = jax.ShapeDtypeStruct((BLK, ROWS), F32)
    dma = pltpu.SemaphoreType.DMA
    outs = pl.pallas_call(
        kernel,
        out_shape=(
            block, block, block,
            jax.ShapeDtypeStruct((EROW, D), F32),
            jax.ShapeDtypeStruct((ROWS, D), BF16),
            small, small, small,
        ),
        in_specs=[pl.BlockSpec(memory_space=pltpu.HBM)] * 9,
        out_specs=[pl.BlockSpec(memory_space=pltpu.VMEM)] * 8,
        scratch_shapes=[
            pltpu.VMEM((ROWS, D), F32),
            pltpu.VMEM((D, ROWS), F32),
            pltpu.VMEM((YS, BLK, ROWS), BF16),
            pltpu.VMEM((YS, BLK, ROWS), BF16),
            pltpu.VMEM((2, HALF, ROWS), BF16),
            pltpu.VMEM((2, HALF, ROWS), BF16),
            pltpu.VMEM((4, HALF, ROWS), BF16),
            pltpu.VMEM((4, HALF, ROWS), BF16),
            pltpu.VMEM((4, HALF, ROWS), BF16),
            pltpu.VMEM((4, HALF, ROWS), BF16),
            pltpu.VMEM((4, HALF, ROWS), BF16),
            pltpu.VMEM((4, HALF, ROWS), BF16),
            pltpu.VMEM((2 * REPS, HALF, ROWS), BF16),
            pltpu.VMEM((D, ROWS), BF16),
            pltpu.VMEM((3, BLK, ROWS), F32),
            pltpu.VMEM((EROW, D), F32),
            pltpu.VMEM((YS, KCONV, CCOL), F32),
            pltpu.VMEM((2, KCONV, CCOL), F32),
            pltpu.VMEM((REPS, KCONV, CCOL), F32),
            pltpu.VMEM((3, KCONV, CCOL), F32),
            pltpu.VMEM((2 * YS, 8, 128), F32),
            pltpu.VMEM((TENS, 8, 128), F32),
            dma((8,)),
            dma, dma((YS,)),
            dma, dma,
            dma((2,)), dma((2,)), dma((2,)),
            dma, dma((2,)),
            dma, dma((6,)),
            dma, dma((3,)),
            dma, dma((3,)),
            dma, dma,
            dma, dma,
            dma, dma,
            dma, dma,
            dma, dma,
            pltpu.SemaphoreType.REGULAR, pltpu.SemaphoreType.REGULAR((2,)),
        ],
        compiler_params=pltpu.CompilerParams(
            collective_id=0, has_side_effects=True, vmem_limit_bytes=48 << 20
        ),
        name="adamw_step",
    )(
        *(
            pltpu.with_memory_space_constraint(x, pltpu.HBM)
            for x in (
                grad_proj[0], grad_conv[0], param_proj.T, m_proj.T, v_proj.T, ema_proj,
                param_conv, m_conv, v_conv,
            )
        )
    )
    outs = pl.pallas_call(
        hand_over,
        out_shape=tuple(jax.ShapeDtypeStruct(x.shape, x.dtype) for x in outs),
        in_specs=[pl.BlockSpec(memory_space=pltpu.VMEM)] * 8,
        out_specs=[pl.BlockSpec(memory_space=pltpu.HBM)] * 8,
        scratch_shapes=[dma((8,))],
        name="hand_over",
    )(*(pltpu.with_memory_space_constraint(x, pltpu.VMEM) for x in outs))
    new_param, new_m, new_v, new_ema, weights, new_cparam, new_cm, new_cv = outs
    return (new_param.T, new_m.T, new_v.T, new_ema, weights, new_cparam, new_cm, new_cv)


def solution(mesh):
    in_specs = (
        P(("rep", "dp"), "tensor", None),
        P(("rep", "dp"), None, "tensor"),
        P("tensor", "dp"),
        P("tensor", "dp"),
        P("tensor", "dp"),
        P(("tensor", "dp"), None),
        P(None, "tensor"),
        P(None, "tensor"),
        P(None, "tensor"),
    )
    out_specs = (
        P("tensor", "dp"),
        P("tensor", "dp"),
        P("tensor", "dp"),
        P(("tensor", "dp"), None),
        P("tensor", None),
        P(None, "tensor"),
        P(None, "tensor"),
        P(None, "tensor"),
    )
    return jax.shard_map(body, mesh=mesh, in_specs=in_specs, out_specs=out_specs, check_vma=False)
```

```python
import functools
import math

import jax
import jax.numpy as jnp
from jax import lax
from jax.experimental import pallas as pl
from jax.experimental.pallas import tpu as pltpu
from jax.sharding import PartitionSpec as P

D = 1536
INNER = 3072
CONV = 3328
KCONV = 4

F32 = jnp.float32
BF16 = jnp.bfloat16
MESH = pl.DeviceIdType.MESH

YS = 8
REPS = 4
TENS = 8
ROWS = INNER // TENS
BLK = D // (2 * YS)
HALF = BLK // 2
CCOL = CONV // TENS
EROW = ROWS // (2 * YS)
SCALE_UP = 2.0**15
SCALE_DOWN = 2.0**-15


def adamw_step(param_in, first_in, second_in, grad_in):
    first_out = 0.9 * first_in + 0.1 * grad_in
    second_out = 0.95 * second_in + 0.05 * grad_in * grad_in
    bias_one = 1.0 - 0.9**10
    bias_two = 1.0 - 0.95**10
    update = first_out / bias_one / (jnp.sqrt(second_out / bias_two) + 1e-08)
    param_out = param_in - 0.25 * (update + 0.1 * param_in)
    return (param_out, first_out, second_out)


def clip_from(square_sum):
    clip_limit = 0.5 * math.sqrt(INNER * D + KCONV * CONV)
    return jnp.minimum(1.0, clip_limit / (jnp.sqrt(square_sum) + 1e-06))


def encode(x):
    wide = x * SCALE_UP
    square = wide * wide
    return ((square * wide) * jnp.abs(wide)).astype(BF16)


def signed_root(x):
    return x * lax.rsqrt(jnp.maximum(jnp.abs(x), 1e-37))


def decode(code):
    return signed_root(signed_root(code.astype(F32))) * SCALE_DOWN


def fold(x):
    total = x[0:8, 0:128]
    for i in range(x.shape[0] // 8):
        for j in range(x.shape[1] // 128):
            if i or j:
                total = total + x[8 * i : 8 * i + 8, 128 * j : 128 * j + 128]
    return total


WAYS = ((1, 0), (-1, 1))


def kernel(
    grad, conv, param, mom, vel, ema, cparam, cmom, cvel,
    o_param, o_mom, o_vel, o_ema, o_weights, o_cparam, o_cmom, o_cvel,
    g_in, gt, pair_out, pair_in, far_out, far_in, mid_out, mid_in, rel_out, rel_in, near_out, near_in,
    zx, wt, state, e_v, conv_y, conv_c, conv_z, cstate, norm_d, norm_t,
    load_sem, pair_s, pair_r, step_s, mid_s, mid_r, rel_r, near_r, zx_s, zx_r,
    own_s, own_r, fwd_s, fwd_r, share_s, share_r, cy_s, cy_r, cc_s, cc_r, cz_s, cz_r,
    nd_s, nd_r, nt_s, nt_r, hello_z, hello_x,
):
    rep = lax.axis_index("rep")
    dp = lax.axis_index("dp")
    ten = lax.axis_index("tensor")
    y = dp // 2
    core = dp % 2
    partner = 2 * y + (1 - core)

    def y_at(off):
        return (y + off + YS) % YS

    def remote(src, dst, send, recv, **device):
        return pltpu.make_async_remote_copy(
            src_ref=src, dst_ref=dst, send_sem=send, recv_sem=recv,
            device_id=device, device_id_type=MESH,
        )

    def sent(ref, sem):
        remote(ref, ref, sem, cc_r, dp=partner).wait_send()

    def landed(ref, sem):
        remote(ref, ref, cc_s, sem, dp=partner).wait_recv()

    def wt_rows(n):
        return wt.at[pl.ds(0, n), :]

    base = (y // 2 + 2) % 4
    turn = 2 * (y % 2) - 1
    order = (base, (base + turn + 4) % 4, (base - turn + 4) % 4, (base + 2) % 4)
    loads = []
    for i, group in enumerate(order):
        cols = pl.ds(pl.multiple_of(group * 384, 128), 384)
        loads.append(pltpu.make_async_copy(grad.at[:, cols], g_in.at[:, cols], load_sem.at[i]))
    for copy in loads:
        copy.start()
    conv_load = pltpu.make_async_copy(conv, conv_z.at[rep], load_sem.at[4])
    late = []
    for src, dst, i in (
        (param, state.at[0], 5), (mom, state.at[1], 5), (vel, state.at[2], 5), (ema, e_v, 6),
        (cparam, cstate.at[0], 7), (cmom, cstate.at[1], 7), (cvel, cstate.at[2], 7),
    ):
        late.append(pltpu.make_async_copy(src, dst, load_sem.at[i]))

    x_near = [{"tensor": (ten + 2) % TENS}, {"tensor": (ten + TENS - 2) % TENS}, {"tensor": ten + 1 - 2 * (ten % 2)}]
    y_near = [{"dp": 2 * y_at(off) + core} for off in (2, -2, 1, -1)]
    barrier = pltpu.get_barrier_semaphore()

    def signal(sem, devices):
        for device in devices:
            pl.semaphore_signal(sem, inc=1, device_id=device, device_id_type=MESH)

    def signal_reps(sem, first, end):
        def step(i, carry):
            pl.semaphore_signal(sem, inc=1, device_id={"rep": i}, device_id_type=MESH)
            return carry

        lax.fori_loop(first, end, step, 0)

    signal(barrier, y_near + x_near + [{"dp": partner}])
    signal_reps(barrier, rep + 1, REPS)

    def turn_group(i):
        loads[i].wait()
        group = order[i]

        def step(j, carry):
            at = pl.multiple_of(group * 384 + j * 128, 128)
            gt[pl.ds(at, 128), :] = g_in[:, pl.ds(at, 128)].T
            return carry

        lax.fori_loop(0, 3, step, 0)
        for k in range(2):
            own = 2 * group + k
            rows = pl.ds(pl.multiple_of((2 * own + (1 - core)) * BLK, BLK), BLK)
            pair_out[own] = encode(gt[rows, :])

    def pair_copy(own):
        return remote(
            pair_out.at[own], pair_in.at[own], pair_s, pair_r.at[own], dp=partner
        )

    def conv_y_copy(off):
        return remote(
            conv_y.at[y], conv_y.at[y], cy_s, cy_r, dp=2 * y_at(off) + core
        )

    for copy in [conv_load] + late:
        copy.start()
    for i in range(4):
        turn_group(i)
    pl.semaphore_wait(barrier, 8 + rep)
    def pair_start(groups):
        for i in groups:
            for k in range(2):
                pair_copy(2 * order[i] + k).start()

    pair_start((0, 1))
    signal_reps(hello_z, 0, rep)
    signal(hello_x.at[0], x_near)

    arrived = set()

    def local_sum(off, half=None):
        own = y_at(off)
        if off % YS not in arrived:
            arrived.add(off % YS)
            pair_copy(own).wait_recv()
        lo, n = (0, BLK) if half is None else (half * HALF, HALF)
        rows = pl.ds(pl.multiple_of((2 * own + core) * BLK + lo, 16), n)
        return gt[rows, :] + decode(pair_in[own, lo : lo + n, :])

    def y_copy(out, into, i, send, recv, hops):
        return remote(out.at[i], into.at[i], send, recv, dp=2 * y_at(hops) + core)

    def far_copy(i):
        return y_copy(far_out, far_in, i, step_s, mid_r.at[i], 2 * WAYS[i][0])

    def mid_copy(i, half):
        send = mid_s if half else step_s
        return y_copy(mid_out, mid_in, 2 * i + half, send, mid_r.at[half], WAYS[i][0])

    def rel_copy(i, half):
        return y_copy(rel_out, rel_in, 2 * i + half, step_s, rel_r.at[half], 2 * WAYS[i][0])

    def near_copy(i, half):
        return y_copy(near_out, near_in, 2 * i + half, step_s, near_r.at[half], WAYS[i][0])

    def conv_c_copy():
        return remote(conv_c.at[core], conv_c.at[core], cc_s, cc_r, dp=partner)

    def conv_z_copy(off):
        return remote(
            conv_z.at[rep], conv_z.at[rep], cz_s, cz_r, rep=(rep + off) % REPS
        )

    for i, (sign, half) in enumerate(WAYS):
        far_out[i] = encode(local_sum(4 * sign, half))
        far_copy(i).start()
    for h in range(2):
        for i, (sign, _) in enumerate(WAYS):
            mid_out[2 * i + h] = encode(local_sum(3 * sign, h))
            mid_copy(i, h).start()
    pair_start((2, 3))
    for h in range(2):
        for i, (sign, _) in enumerate(WAYS):
            near_out[2 * i + h] = encode(local_sum(sign, h))
    sent(wt_rows(2 * HALF), mid_s)
    for h in range(2):
        for i in range(2):
            near_copy(i, h).start()
    for i, h in ((0, 0), (1, 0), (1, 1), (0, 1)):
        if i == h:
            landed(wt_rows(3 * HALF), mid_r.at[h])
        total = local_sum(2 * WAYS[i][0], h) + decode(mid_in[2 * i + h])
        if h == WAYS[i][1]:
            total = total + decode(far_in[i])
        rel_out[2 * i + h] = encode(total)
        rel_copy(i, h).start()
    conv_load.wait()
    @pl.when(rep < REPS - 1)
    def _():
        pl.semaphore_wait(hello_z, REPS - 1 - rep)

    for off in range(1, REPS):
        conv_z_copy(off).start()
    pl.semaphore_wait(hello_x.at[0], 3)
    signal(hello_x.at[1], x_near)

    def zx_copy(off, h):
        return remote(
            zx.at[2 * rep + h], zx.at[2 * rep + h], zx_s, zx_r.at[h],
            rep=(rep + off) % REPS,
        )

    for h in range(2):
        total = local_sum(0, h)
        landed(near_in.at[pl.ds(0, 2)], near_r.at[h])
        for i in range(2):
            total = total + decode(near_in[2 * i + h])
        landed(rel_in.at[pl.ds(0, 2)], rel_r.at[h])
        for i in range(2):
            total = total + decode(rel_in[2 * i + h])
        zx[2 * rep + h] = encode(total)
        for off in (2, 1, 3):
            zx_copy(off, h).start()

    count = float(REPS * 2 * YS)
    landed(conv_z.at[pl.ds(0, REPS - 1)], cz_r)
    conv_y[y] = ((conv_z[0] + conv_z[1]) + conv_z[2]) + conv_z[3]
    for off in range(1, YS):
        conv_y_copy(off).start()

    avg = []
    for h in range(2):
        landed(zx.at[pl.ds(0, REPS - 1)], zx_r.at[h])
        total = decode(zx[h])
        for r in range(1, REPS):
            total = total + decode(zx[2 * r + h])
        avg.append(total * (1.0 / count))
        if h == 0:
            landed(conv_y.at[pl.ds(0, YS - 1)], cy_r)
            total = conv_y[0]
            for i in range(1, YS):
                total = total + conv_y[i]
            conv_c[core] = total
            conv_c_copy().start()

    def rows_at(buf, first, n):
        return buf.at[pl.ds(first, n), pl.ds(0, 1), :]

    def spread(buf, send, recv, axis, me, size):
        at = rows_at(buf, me, 1)
        for i in sorted(range(1, size), key=lambda i: abs(i - size // 2)):
            remote(at, at, send, recv, **{axis: (me + i) % size}).start()

    def collect(buf, recv, size):
        landed(rows_at(buf, 0, size - 1), recv)
        total = buf[0, 0:1, :]
        for i in range(1, size):
            total = total + buf[i, 0:1, :]
        return total

    square = fold(avg[0] * avg[0]) + fold(avg[1] * avg[1])
    norm_d[dp, 0:1, :] = jnp.sum(square, axis=0, keepdims=True)
    spread(norm_d, nd_s, nd_r, "dp", dp, 2 * YS)
    for h in range(2):
        gt[h * HALF : (h + 1) * HALF, :] = avg[h]
    for ref, i in ((state, 5), (e_v, 6), (cstate, 7)):
        pltpu.make_async_copy(ref, ref, load_sem.at[i]).wait()
    conv_c_copy().wait_recv()
    conv_avg = (conv_c[0] + conv_c[1]) * (1.0 / count)
    conv_square = jnp.sum(conv_avg * conv_avg)
    pl.semaphore_wait(hello_x.at[1], 3)
    norm_t[ten, 0:1, :] = collect(norm_d, nd_r, 2 * YS) + conv_square * (1.0 / 128.0)
    spread(norm_t, nt_s, nt_r, "tensor", ten, TENS)

    square_sum = jnp.sum(collect(norm_t, nt_r, TENS), keepdims=True)
    clip = clip_from(square_sum)

    new_param, new_mom, new_vel = adamw_step(state[0], state[1], state[2], clip * gt[0:BLK, :])
    mine = pl.multiple_of(dp * BLK, BLK)
    wt[pl.ds(mine, BLK), :] = new_param.astype(BF16)

    def rows_of(off, whose, half=None):
        lo, n = (0, BLK) if half is None else (half * HALF, HALF)
        return pl.ds(pl.multiple_of((2 * y_at(off) + whose) * BLK + lo, 16), n)

    def gather_copy(send, recv, slot, off, half, hops):
        rows = rows_of(off, core, half)
        return remote(
            wt.at[rows, :], wt.at[rows, :], send, recv.at[slot], dp=2 * y_at(hops) + core
        )

    def own2_copy(i, half):
        return gather_copy(own_s, own_r, 2 * i + half, 0, half, 2 * WAYS[i][0])

    def own1_copy(i):
        return gather_copy(fwd_s, own_r, 4 + i, 0, None, WAYS[i][0])

    def fwd1_copy(i, half):
        return gather_copy(fwd_s, fwd_r, half if i == 0 else 1 - half, -2 * WAYS[i][0], half, WAYS[i][0])

    def fwd2_copy(i):
        sign, half = WAYS[i]
        return gather_copy(fwd_s, fwd_r, 2, -2 * sign, half, 2 * sign)

    def share_copy(off, half):
        rows = rows_of(off, core, half)
        slot = 0 if abs(off) <= 2 else 2 if off == 4 else (3 - turn * (-off // 3)) // 2
        return remote(wt.at[rows, :], wt.at[rows, :], share_s, share_r.at[slot], dp=partner)

    for k in range(2):
        for i, (sign, half) in enumerate(WAYS):
            own2_copy(i, half if k == 0 else 1 - half).start()
    share_copy(0, None).start()

    o_param[...] = new_param
    o_mom[...] = new_mom
    o_vel[...] = new_vel
    new_cparam, new_cmom, new_cvel = adamw_step(cstate[0], cstate[1], cstate[2], clip * conv_avg)
    o_cparam[...] = new_cparam
    o_cmom[...] = new_cmom
    o_cvel[...] = new_cvel

    sent(wt_rows(4 * HALF), own_s)
    for i in range(2):
        own1_copy(i).start()

    sent(pair_out, pair_s)
    sent(wt_rows(12 * HALF), step_s)
    sent(conv_y.at[pl.ds(0, YS - 1)], cy_s)
    conv_c_copy().wait_send()
    sent(conv_z.at[pl.ds(0, REPS - 1)], cz_s)
    sent(zx.at[pl.ds(0, 2 * (REPS - 1))], zx_s)
    sent(rows_at(norm_d, 0, 2 * YS - 1), nd_s)
    sent(rows_at(norm_t, 0, TENS - 1), nt_s)

    for k in range(2):
        for i, (sign, half) in enumerate(WAYS):
            h = half if k == 0 else 1 - half
            own2_copy(i, h).wait_recv()
            if k == 0:
                fwd2_copy(i).start()
            fwd1_copy(i, h).start()
            share_copy(-2 * sign, h).start()
    for i, (sign, _) in enumerate(WAYS):
        own1_copy(i).wait_recv()
        share_copy(-sign, None).start()

    def back(first):
        def step(j, carry):
            at = pl.multiple_of(first * 192 + j * 128, 128)
            o_weights[:, pl.ds(at, 128)] = wt[pl.ds(at, 128), :].T
            return carry

        lax.fori_loop(0, 3, step, 0)

    landed(wt_rows(2 * HALF), fwd_r.at[2])
    for i, (_, half) in enumerate(WAYS):
        share_copy(4, half).start()
    for k in range(2):
        landed(wt_rows(2 * HALF), fwd_r.at[k])
        for i, (sign, half) in enumerate(WAYS):
            share_copy(-3 * sign, half if k == 0 else 1 - half).start()
    landed(wt_rows(5 * BLK), share_r.at[0])
    pair = y // 2
    back(2 * pair)
    back(2 * ((pair + turn + 4) % 4))
    landed(wt_rows(BLK), share_r.at[1])
    back(2 * ((pair - turn + 4) % 4))
    landed(wt_rows(2 * BLK), share_r.at[2])
    back(2 * ((pair + 2) % 4))
    near = o_weights[pl.ds(pl.multiple_of(y * 2 * EROW, 16), 2 * EROW), :].astype(F32)
    row_block = jnp.where(core == 0, near[0:EROW], near[EROW:])
    o_ema[...] = 0.9 * e_v[...] + 0.1 * row_block

    sent(wt_rows(10 * HALF), fwd_s)
    sent(wt_rows(8 * BLK), share_s)


def hand_over(*refs):
    sems = refs[-1]
    copies = [
        pltpu.make_async_copy(refs[i], refs[8 + i], sems.at[i]) for i in (4, 0, 1, 2, 3, 5, 6, 7)
    ]
    for copy in copies:
        copy.start()
    for copy in copies:
        copy.wait()


def body(grad_proj, grad_conv, param_proj, m_proj, v_proj, ema_proj, param_conv, m_conv, v_conv):
    small = jax.ShapeDtypeStruct((KCONV, CCOL), F32)
    block = jax.ShapeDtypeStruct((BLK, ROWS), F32)
    dma = pltpu.SemaphoreType.DMA
    outs = pl.pallas_call(
        kernel,
        out_shape=(
            block, block, block,
            jax.ShapeDtypeStruct((EROW, D), F32),
            jax.ShapeDtypeStruct((ROWS, D), BF16),
            small, small, small,
        ),
        in_specs=[pl.BlockSpec(memory_space=pltpu.HBM)] * 9,
        out_specs=[pl.BlockSpec(memory_space=pltpu.VMEM)] * 8,
        scratch_shapes=[
            pltpu.VMEM((ROWS, D), F32),
            pltpu.VMEM((D, ROWS), F32),
            pltpu.VMEM((YS, BLK, ROWS), BF16),
            pltpu.VMEM((YS, BLK, ROWS), BF16),
            pltpu.VMEM((2, HALF, ROWS), BF16),
            pltpu.VMEM((2, HALF, ROWS), BF16),
            pltpu.VMEM((4, HALF, ROWS), BF16),
            pltpu.VMEM((4, HALF, ROWS), BF16),
            pltpu.VMEM((4, HALF, ROWS), BF16),
            pltpu.VMEM((4, HALF, ROWS), BF16),
            pltpu.VMEM((4, HALF, ROWS), BF16),
            pltpu.VMEM((4, HALF, ROWS), BF16),
            pltpu.VMEM((2 * REPS, HALF, ROWS), BF16),
            pltpu.VMEM((D, ROWS), BF16),
            pltpu.VMEM((3, BLK, ROWS), F32),
            pltpu.VMEM((EROW, D), F32),
            pltpu.VMEM((YS, KCONV, CCOL), F32),
            pltpu.VMEM((2, KCONV, CCOL), F32),
            pltpu.VMEM((REPS, KCONV, CCOL), F32),
            pltpu.VMEM((3, KCONV, CCOL), F32),
            pltpu.VMEM((2 * YS, 8, 128), F32),
            pltpu.VMEM((TENS, 8, 128), F32),
            dma((8,)),
            dma, dma((YS,)),
            dma, dma,
            dma((2,)), dma((2,)), dma((2,)),
            dma, dma((2,)),
            dma, dma((6,)),
            dma, dma((3,)),
            dma, dma((3,)),
            dma, dma,
            dma, dma,
            dma, dma,
            dma, dma,
            dma, dma,
            pltpu.SemaphoreType.REGULAR, pltpu.SemaphoreType.REGULAR((2,)),
        ],
        compiler_params=pltpu.CompilerParams(
            collective_id=0, has_side_effects=True, vmem_limit_bytes=48 << 20
        ),
        name="adamw_step",
    )(
        *(
            pltpu.with_memory_space_constraint(x, pltpu.HBM)
            for x in (
                grad_proj[0], grad_conv[0], param_proj.T, m_proj.T, v_proj.T, ema_proj,
                param_conv, m_conv, v_conv,
            )
        )
    )
    outs = pl.pallas_call(
        hand_over,
        out_shape=tuple(jax.ShapeDtypeStruct(x.shape, x.dtype) for x in outs),
        in_specs=[pl.BlockSpec(memory_space=pltpu.VMEM)] * 8,
        out_specs=[pl.BlockSpec(memory_space=pltpu.HBM)] * 8,
        scratch_shapes=[dma((8,))],
        name="hand_over",
    )(*(pltpu.with_memory_space_constraint(x, pltpu.VMEM) for x in outs))
    new_param, new_m, new_v, new_ema, weights, new_cparam, new_cm, new_cv = outs
    return (new_param.T, new_m.T, new_v.T, new_ema, weights, new_cparam, new_cm, new_cv)


def solution(mesh):
    in_specs = (
        P(("rep", "dp"), "tensor", None),
        P(("rep", "dp"), None, "tensor"),
        P("tensor", "dp"),
        P("tensor", "dp"),
        P("tensor", "dp"),
        P(("tensor", "dp"), None),
        P(None, "tensor"),
        P(None, "tensor"),
        P(None, "tensor"),
    )
    out_specs = (
        P("tensor", "dp"),
        P("tensor", "dp"),
        P("tensor", "dp"),
        P(("tensor", "dp"), None),
        P("tensor", None),
        P(None, "tensor"),
        P(None, "tensor"),
        P(None, "tensor"),
    )
    return jax.shard_map(body, mesh=mesh, in_specs=in_specs, out_specs=out_specs, check_vma=False)
```

```python
import functools
import math

import jax
import jax.numpy as jnp
from jax import lax
from jax.experimental import pallas as pl
from jax.experimental.pallas import tpu as pltpu
from jax.sharding import PartitionSpec as P

D = 1536
INNER = 3072
CONV = 3328
KCONV = 4

F32 = jnp.float32
BF16 = jnp.bfloat16
MESH = pl.DeviceIdType.MESH

YS = 8
REPS = 4
TENS = 8
ROWS = INNER // TENS
BLK = D // (2 * YS)
HALF = BLK // 2
CCOL = CONV // TENS
EROW = ROWS // (2 * YS)
SCALE_UP = 2.0**15
SCALE_DOWN = 2.0**-15


def adamw_step(param_in, first_in, second_in, grad_in):
    first_out = 0.9 * first_in + 0.1 * grad_in
    second_out = 0.95 * second_in + 0.05 * grad_in * grad_in
    bias_one = 1.0 - 0.9**10
    bias_two = 1.0 - 0.95**10
    update = first_out / bias_one / (jnp.sqrt(second_out / bias_two) + 1e-08)
    param_out = param_in - 0.25 * (update + 0.1 * param_in)
    return (param_out, first_out, second_out)


def clip_from(square_sum):
    clip_limit = 0.5 * math.sqrt(INNER * D + KCONV * CONV)
    return jnp.minimum(1.0, clip_limit / (jnp.sqrt(square_sum) + 1e-06))


def encode(x):
    wide = x * SCALE_UP
    square = wide * wide
    return ((square * wide) * jnp.abs(wide)).astype(BF16)


def signed_root(x):
    return x * lax.rsqrt(jnp.maximum(jnp.abs(x), 1e-37))


def decode(code):
    return signed_root(signed_root(code.astype(F32))) * SCALE_DOWN


def fold(x):
    total = x[0:8, 0:128]
    for i in range(x.shape[0] // 8):
        for j in range(x.shape[1] // 128):
            if i or j:
                total = total + x[8 * i : 8 * i + 8, 128 * j : 128 * j + 128]
    return total


WAYS = ((1, 0), (-1, 1))


def kernel(
    grad, conv, param, mom, vel, ema, cparam, cmom, cvel,
    o_param, o_mom, o_vel, o_ema, o_weights, o_cparam, o_cmom, o_cvel,
    g_in, gt, pair_out, pair_in, far_out, far_in, mid_out, mid_in, rel_out, rel_in, near_out, near_in,
    zx, wt, state, e_v, conv_y, conv_c, conv_z, cstate, norm_d, norm_t,
    load_sem, pair_s, pair_r, step_s, mid_s, mid_r, rel_r, near_r, zx_s, zx_r,
    own_s, own_r, fwd_s, fwd_r, share_s, share_r, cy_s, cy_r, cc_s, cc_r, cz_s, cz_r,
    nd_s, nd_r, nt_s, nt_r, hello_z, hello_x,
):
    rep = lax.axis_index("rep")
    dp = lax.axis_index("dp")
    ten = lax.axis_index("tensor")
    y = dp // 2
    core = dp % 2
    partner = 2 * y + (1 - core)

    def y_at(off):
        return (y + off + YS) % YS

    def remote(src, dst, send, recv, **device):
        return pltpu.make_async_remote_copy(
            src_ref=src, dst_ref=dst, send_sem=send, recv_sem=recv,
            device_id=device, device_id_type=MESH,
        )

    def sent(ref, sem):
        remote(ref, ref, sem, cc_r, dp=partner).wait_send()

    def landed(ref, sem):
        remote(ref, ref, cc_s, sem, dp=partner).wait_recv()

    def wt_rows(n):
        return wt.at[pl.ds(0, n), :]

    base = (y // 2 + 2) % 4
    turn = 2 * (y % 2) - 1
    order = (base, (base + turn + 4) % 4, (base - turn + 4) % 4, (base + 2) % 4)
    loads = []
    for i, group in enumerate(order):
        cols = pl.ds(pl.multiple_of(group * 384, 128), 384)
        loads.append(pltpu.make_async_copy(grad.at[:, cols], g_in.at[:, cols], load_sem.at[i]))
    for copy in loads:
        copy.start()
    conv_load = pltpu.make_async_copy(conv, conv_z.at[rep], load_sem.at[4])
    late = []
    for src, dst, i in (
        (param, state.at[0], 5), (mom, state.at[1], 5), (vel, state.at[2], 5), (ema, e_v, 6),
        (cparam, cstate.at[0], 7), (cmom, cstate.at[1], 7), (cvel, cstate.at[2], 7),
    ):
        late.append(pltpu.make_async_copy(src, dst, load_sem.at[i]))

    x_near = [{"tensor": (ten + 2) % TENS}, {"tensor": (ten + TENS - 2) % TENS}, {"tensor": ten + 1 - 2 * (ten % 2)}]
    y_near = [{"dp": 2 * y_at(off) + core} for off in (2, -2, 1, -1)]
    barrier = pltpu.get_barrier_semaphore()

    def signal(sem, devices):
        for device in devices:
            pl.semaphore_signal(sem, inc=1, device_id=device, device_id_type=MESH)

    def signal_reps(sem, first, end):
        def step(i, carry):
            pl.semaphore_signal(sem, inc=1, device_id={"rep": i}, device_id_type=MESH)
            return carry

        lax.fori_loop(first, end, step, 0)

    signal(barrier, y_near + x_near + [{"dp": partner}])
    signal_reps(barrier, rep + 1, REPS)

    def turn_group(i):
        loads[i].wait()
        group = order[i]

        def step(j, carry):
            at = pl.multiple_of(group * 384 + j * 128, 128)
            gt[pl.ds(at, 128), :] = g_in[:, pl.ds(at, 128)].T
            return carry

        lax.fori_loop(0, 3, step, 0)
        for k in range(2):
            own = 2 * group + k
            rows = pl.ds(pl.multiple_of((2 * own + (1 - core)) * BLK, BLK), BLK)
            pair_out[own] = encode(gt[rows, :])

    def pair_copy(own):
        return remote(
            pair_out.at[own], pair_in.at[own], pair_s, pair_r.at[own], dp=partner
        )

    def conv_y_copy(off):
        return remote(
            conv_y.at[y], conv_y.at[y], cy_s, cy_r, dp=2 * y_at(off) + core
        )

    for copy in [conv_load] + late:
        copy.start()
    for i in range(4):
        turn_group(i)
    pl.semaphore_wait(barrier, 8 + rep)
    def pair_start(groups):
        for i in groups:
            for k in range(2):
                pair_copy(2 * order[i] + k).start()

    pair_start((0, 1))
    signal_reps(hello_z, 0, rep)
    signal(hello_x.at[0], x_near)

    arrived = set()

    def local_sum(off, half=None):
        own = y_at(off)
        if off % YS not in arrived:
            arrived.add(off % YS)
            pair_copy(own).wait_recv()
        lo, n = (0, BLK) if half is None else (half * HALF, HALF)
        rows = pl.ds(pl.multiple_of((2 * own + core) * BLK + lo, 16), n)
        return gt[rows, :] + decode(pair_in[own, lo : lo + n, :])

    def y_copy(out, into, i, send, recv, hops):
        return remote(out.at[i], into.at[i], send, recv, dp=2 * y_at(hops) + core)

    def far_copy(i):
        return y_copy(far_out, far_in, i, step_s, mid_r.at[i], 2 * WAYS[i][0])

    def mid_copy(i, half):
        send = mid_s if half else step_s
        return y_copy(mid_out, mid_in, 2 * i + half, send, mid_r.at[half], WAYS[i][0])

    def rel_copy(i, half):
        return y_copy(rel_out, rel_in, 2 * i + half, step_s, rel_r.at[half], 2 * WAYS[i][0])

    def near_copy(i, half):
        return y_copy(near_out, near_in, 2 * i + half, step_s, near_r.at[half], WAYS[i][0])

    def conv_c_copy():
        return remote(conv_c.at[core], conv_c.at[core], cc_s, cc_r, dp=partner)

    def conv_z_copy(off):
        return remote(
            conv_z.at[rep], conv_z.at[rep], cz_s, cz_r, rep=(rep + off) % REPS
        )

    for i, (sign, half) in enumerate(WAYS):
        far_out[i] = encode(local_sum(4 * sign, half))
        far_copy(i).start()
    for h in range(2):
        for i, (sign, _) in enumerate(WAYS):
            mid_out[2 * i + h] = encode(local_sum(3 * sign, h))
            mid_copy(i, h).start()
    pair_start((2, 3))
    for h in range(2):
        for i, (sign, _) in enumerate(WAYS):
            near_out[2 * i + h] = encode(local_sum(sign, h))
    sent(wt_rows(2 * HALF), mid_s)
    for h in range(2):
        for i in range(2):
            near_copy(i, h).start()
    for i, h in ((0, 0), (1, 0), (1, 1), (0, 1)):
        if i == h:
            landed(wt_rows(3 * HALF), mid_r.at[h])
        total = local_sum(2 * WAYS[i][0], h) + decode(mid_in[2 * i + h])
        if h == WAYS[i][1]:
            total = total + decode(far_in[i])
        rel_out[2 * i + h] = encode(total)
        rel_copy(i, h).start()
    conv_load.wait()
    @pl.when(rep < REPS - 1)
    def _():
        pl.semaphore_wait(hello_z, REPS - 1 - rep)

    for off in range(1, REPS):
        conv_z_copy(off).start()
    pl.semaphore_wait(hello_x.at[0], 3)
    signal(hello_x.at[1], x_near)

    def zx_copy(off, h):
        return remote(
            zx.at[2 * rep + h], zx.at[2 * rep + h], zx_s, zx_r.at[h],
            rep=(rep + off) % REPS,
        )

    for h in range(2):
        total = local_sum(0, h)
        landed(near_in.at[pl.ds(0, 2)], near_r.at[h])
        for i in range(2):
            total = total + decode(near_in[2 * i + h])
        landed(rel_in.at[pl.ds(0, 2)], rel_r.at[h])
        for i in range(2):
            total = total + decode(rel_in[2 * i + h])
        zx[2 * rep + h] = encode(total)
        for off in (2, 1, 3):
            zx_copy(off, h).start()

    count = float(REPS * 2 * YS)
    landed(conv_z.at[pl.ds(0, REPS - 1)], cz_r)
    conv_y[y] = ((conv_z[0] + conv_z[1]) + conv_z[2]) + conv_z[3]
    for off in range(1, YS):
        conv_y_copy(off).start()

    avg = []
    for h in range(2):
        landed(zx.at[pl.ds(0, REPS - 1)], zx_r.at[h])
        total = decode(zx[h])
        for r in range(1, REPS):
            total = total + decode(zx[2 * r + h])
        avg.append(total * (1.0 / count))
        if h == 0:
            landed(conv_y.at[pl.ds(0, YS - 1)], cy_r)
            total = conv_y[0]
            for i in range(1, YS):
                total = total + conv_y[i]
            conv_c[core] = total
            conv_c_copy().start()

    def rows_at(buf, first, n):
        return buf.at[pl.ds(first, n), pl.ds(0, 1), :]

    def spread(buf, send, recv, axis, me, size):
        at = rows_at(buf, me, 1)
        for i in sorted(range(1, size), key=lambda i: abs(i - size // 2)):
            remote(at, at, send, recv, **{axis: (me + i) % size}).start()

    def collect(buf, recv, size):
        landed(rows_at(buf, 0, size - 1), recv)
        total = buf[0, 0:1, :]
        for i in range(1, size):
            total = total + buf[i, 0:1, :]
        return total

    square = fold(avg[0] * avg[0]) + fold(avg[1] * avg[1])
    norm_d[dp, 0:1, :] = jnp.sum(square, axis=0, keepdims=True)
    spread(norm_d, nd_s, nd_r, "dp", dp, 2 * YS)
    for h in range(2):
        gt[h * HALF : (h + 1) * HALF, :] = avg[h]
    for ref, i in ((state, 5), (e_v, 6), (cstate, 7)):
        pltpu.make_async_copy(ref, ref, load_sem.at[i]).wait()
    conv_c_copy().wait_recv()
    conv_avg = (conv_c[0] + conv_c[1]) * (1.0 / count)
    conv_square = jnp.sum(conv_avg * conv_avg)
    pl.semaphore_wait(hello_x.at[1], 3)
    norm_t[ten, 0:1, :] = collect(norm_d, nd_r, 2 * YS) + conv_square * (1.0 / 128.0)
    spread(norm_t, nt_s, nt_r, "tensor", ten, TENS)

    square_sum = jnp.sum(collect(norm_t, nt_r, TENS), keepdims=True)
    clip = clip_from(square_sum)

    new_param, new_mom, new_vel = adamw_step(state[0], state[1], state[2], clip * gt[0:BLK, :])
    mine = pl.multiple_of(dp * BLK, BLK)
    wt[pl.ds(mine, BLK), :] = new_param.astype(BF16)

    def rows_of(off, whose, half=None):
        lo, n = (0, BLK) if half is None else (half * HALF, HALF)
        return pl.ds(pl.multiple_of((2 * y_at(off) + whose) * BLK + lo, 16), n)

    def gather_copy(send, recv, slot, off, half, hops):
        rows = rows_of(off, core, half)
        return remote(
            wt.at[rows, :], wt.at[rows, :], send, recv.at[slot], dp=2 * y_at(hops) + core
        )

    def own2_copy(i, half):
        return gather_copy(own_s, own_r, 2 * i + half, 0, half, 2 * WAYS[i][0])

    def own1_copy(i):
        return gather_copy(fwd_s, own_r, 4 + i, 0, None, WAYS[i][0])

    def fwd1_copy(i, half):
        return gather_copy(fwd_s, fwd_r, half if i == 0 else 1 - half, -2 * WAYS[i][0], half, WAYS[i][0])

    def fwd2_copy(i):
        sign, half = WAYS[i]
        return gather_copy(fwd_s, fwd_r, 2, -2 * sign, half, 2 * sign)

    def share_copy(off, half):
        rows = rows_of(off, core, half)
        slot = 0 if abs(off) <= 2 else 2 if off == 4 else (3 - turn * (-off // 3)) // 2
        return remote(wt.at[rows, :], wt.at[rows, :], share_s, share_r.at[slot], dp=partner)

    for k in range(2):
        for i, (sign, half) in enumerate(WAYS):
            own2_copy(i, half if k == 0 else 1 - half).start()
    share_copy(0, None).start()

    o_param[...] = new_param
    o_mom[...] = new_mom
    o_vel[...] = new_vel
    new_cparam, new_cmom, new_cvel = adamw_step(cstate[0], cstate[1], cstate[2], clip * conv_avg)
    o_cparam[...] = new_cparam
    o_cmom[...] = new_cmom
    o_cvel[...] = new_cvel

    for i in range(2):
        own1_copy(i).start()

    sent(pair_out, pair_s)
    sent(wt_rows(12 * HALF), step_s)
    sent(conv_y.at[pl.ds(0, YS - 1)], cy_s)
    conv_c_copy().wait_send()
    sent(conv_z.at[pl.ds(0, REPS - 1)], cz_s)
    sent(zx.at[pl.ds(0, 2 * (REPS - 1))], zx_s)
    sent(rows_at(norm_d, 0, 2 * YS - 1), nd_s)
    sent(rows_at(norm_t, 0, TENS - 1), nt_s)

    for k in range(2):
        for i, (sign, half) in enumerate(WAYS):
            h = half if k == 0 else 1 - half
            own2_copy(i, h).wait_recv()
            if k == 0:
                fwd2_copy(i).start()
            fwd1_copy(i, h).start()
            share_copy(-2 * sign, h).start()
    for i, (sign, _) in enumerate(WAYS):
        own1_copy(i).wait_recv()
        share_copy(-sign, None).start()

    def back(first):
        def step(j, carry):
            at = pl.multiple_of(first * 192 + j * 128, 128)
            o_weights[:, pl.ds(at, 128)] = wt[pl.ds(at, 128), :].T
            return carry

        lax.fori_loop(0, 3, step, 0)

    landed(wt_rows(2 * HALF), fwd_r.at[2])
    for i, (_, half) in enumerate(WAYS):
        share_copy(4, half).start()
    for k in range(2):
        landed(wt_rows(2 * HALF), fwd_r.at[k])
        for i, (sign, half) in enumerate(WAYS):
            share_copy(-3 * sign, half if k == 0 else 1 - half).start()
    landed(wt_rows(5 * BLK), share_r.at[0])
    pair = y // 2
    back(2 * pair)
    back(2 * ((pair + turn + 4) % 4))
    landed(wt_rows(BLK), share_r.at[1])
    back(2 * ((pair - turn + 4) % 4))
    landed(wt_rows(2 * BLK), share_r.at[2])
    back(2 * ((pair + 2) % 4))
    near = o_weights[pl.ds(pl.multiple_of(y * 2 * EROW, 16), 2 * EROW), :].astype(F32)
    row_block = jnp.where(core == 0, near[0:EROW], near[EROW:])
    o_ema[...] = 0.9 * e_v[...] + 0.1 * row_block

    sent(wt_rows(4 * HALF), own_s)
    sent(wt_rows(10 * HALF), fwd_s)
    sent(wt_rows(8 * BLK), share_s)


def hand_over(*refs):
    sems = refs[-1]
    copies = [
        pltpu.make_async_copy(refs[i], refs[8 + i], sems.at[i]) for i in (4, 0, 1, 2, 3, 5, 6, 7)
    ]
    for copy in copies:
        copy.start()
    for copy in copies:
        copy.wait()


def body(grad_proj, grad_conv, param_proj, m_proj, v_proj, ema_proj, param_conv, m_conv, v_conv):
    small = jax.ShapeDtypeStruct((KCONV, CCOL), F32)
    block = jax.ShapeDtypeStruct((BLK, ROWS), F32)
    dma = pltpu.SemaphoreType.DMA
    outs = pl.pallas_call(
        kernel,
        out_shape=(
            block, block, block,
            jax.ShapeDtypeStruct((EROW, D), F32),
            jax.ShapeDtypeStruct((ROWS, D), BF16),
            small, small, small,
        ),
        in_specs=[pl.BlockSpec(memory_space=pltpu.HBM)] * 9,
        out_specs=[pl.BlockSpec(memory_space=pltpu.VMEM)] * 8,
        scratch_shapes=[
            pltpu.VMEM((ROWS, D), F32),
            pltpu.VMEM((D, ROWS), F32),
            pltpu.VMEM((YS, BLK, ROWS), BF16),
            pltpu.VMEM((YS, BLK, ROWS), BF16),
            pltpu.VMEM((2, HALF, ROWS), BF16),
            pltpu.VMEM((2, HALF, ROWS), BF16),
            pltpu.VMEM((4, HALF, ROWS), BF16),
            pltpu.VMEM((4, HALF, ROWS), BF16),
            pltpu.VMEM((4, HALF, ROWS), BF16),
            pltpu.VMEM((4, HALF, ROWS), BF16),
            pltpu.VMEM((4, HALF, ROWS), BF16),
            pltpu.VMEM((4, HALF, ROWS), BF16),
            pltpu.VMEM((2 * REPS, HALF, ROWS), BF16),
            pltpu.VMEM((D, ROWS), BF16),
            pltpu.VMEM((3, BLK, ROWS), F32),
            pltpu.VMEM((EROW, D), F32),
            pltpu.VMEM((YS, KCONV, CCOL), F32),
            pltpu.VMEM((2, KCONV, CCOL), F32),
            pltpu.VMEM((REPS, KCONV, CCOL), F32),
            pltpu.VMEM((3, KCONV, CCOL), F32),
            pltpu.VMEM((2 * YS, 8, 128), F32),
            pltpu.VMEM((TENS, 8, 128), F32),
            dma((8,)),
            dma, dma((YS,)),
            dma, dma,
            dma((2,)), dma((2,)), dma((2,)),
            dma, dma((2,)),
            dma, dma((6,)),
            dma, dma((3,)),
            dma, dma((3,)),
            dma, dma,
            dma, dma,
            dma, dma,
            dma, dma,
            dma, dma,
            pltpu.SemaphoreType.REGULAR, pltpu.SemaphoreType.REGULAR((2,)),
        ],
        compiler_params=pltpu.CompilerParams(
            collective_id=0, has_side_effects=True, vmem_limit_bytes=48 << 20
        ),
        name="adamw_step",
    )(
        *(
            pltpu.with_memory_space_constraint(x, pltpu.HBM)
            for x in (
                grad_proj[0], grad_conv[0], param_proj.T, m_proj.T, v_proj.T, ema_proj,
                param_conv, m_conv, v_conv,
            )
        )
    )
    outs = pl.pallas_call(
        hand_over,
        out_shape=tuple(jax.ShapeDtypeStruct(x.shape, x.dtype) for x in outs),
        in_specs=[pl.BlockSpec(memory_space=pltpu.VMEM)] * 8,
        out_specs=[pl.BlockSpec(memory_space=pltpu.HBM)] * 8,
        scratch_shapes=[dma((8,))],
        name="hand_over",
    )(*(pltpu.with_memory_space_constraint(x, pltpu.VMEM) for x in outs))
    new_param, new_m, new_v, new_ema, weights, new_cparam, new_cm, new_cv = outs
    return (new_param.T, new_m.T, new_v.T, new_ema, weights, new_cparam, new_cm, new_cv)


def solution(mesh):
    in_specs = (
        P(("rep", "dp"), "tensor", None),
        P(("rep", "dp"), None, "tensor"),
        P("tensor", "dp"),
        P("tensor", "dp"),
        P("tensor", "dp"),
        P(("tensor", "dp"), None),
        P(None, "tensor"),
        P(None, "tensor"),
        P(None, "tensor"),
    )
    out_specs = (
        P("tensor", "dp"),
        P("tensor", "dp"),
        P("tensor", "dp"),
        P(("tensor", "dp"), None),
        P("tensor", None),
        P(None, "tensor"),
        P(None, "tensor"),
        P(None, "tensor"),
    )
    return jax.shard_map(body, mesh=mesh, in_specs=in_specs, out_specs=out_specs, check_vma=False)
```
